256 devices in a mesh: dp: 128 (over x, z_lo, y, core), tensor: 2 (over z_hi).
Axes of the slice: x: 4, y: 4, z: 8 (z_hi: 2, z_lo: 4; z = z_hi * 4 + z_lo), core: 2. Of those that a mesh axis runs over, the one named last changes fastest.
Arguments:
- tokens: bfloat16 [2, 256, 128, 1536], P(None, 'tensor', 'dp'), may hold values from -6 to 6
- cotangent: bfloat16 [2, 256, 128, 1536], P(None, 'tensor', 'dp'), may hold values from -6 to 6
- lengths: int32 [2, 256], replicated, may hold values from 1 to 128, 24576 in all within a row
- perm: int32 [2, 2, 128], replicated, may hold values from 0 to 127, each once within a row
- routes: int32 [2, 256, 128, 6], P(None, None, 'dp'), may hold values from 0 to 7, all different within a row
- gain_attn: float32 [1536], replicated, may hold values from 0.5 to 1.5
- gain_ffn: float32 [1536], replicated, may hold values from 0.5 to 1.5
- query_matrix: bfloat16 [1536, 1536], P('dp', 'tensor'), may hold values from -0.15625 to 0.15625
- key_matrix: bfloat16 [1536, 512], P('dp', 'tensor'), may hold values from -0.15625 to 0.15625
- value_matrix: bfloat16 [1536, 512], P('dp', 'tensor'), may hold values from -0.15625 to 0.15625
- w_out: bfloat16 [1536, 1536], P('tensor', 'dp'), may hold values from -0.875 to 0.875
- w_router: bfloat16 [1536, 8], replicated, may hold values from -0.078125 to 0.078125
- w_gate: bfloat16 [8, 1536, 512], P(None, 'dp', 'tensor'), may hold values from -0.15625 to 0.15625
- w_up: bfloat16 [8, 1536, 512], P(None, 'dp', 'tensor'), may hold values from -0.15625 to 0.15625
- w_down: bfloat16 [8, 512, 1536], P(None, 'tensor', 'dp'), may hold values from -0.75 to 0.75
- s_gate: bfloat16 [1536, 1024], P('dp', 'tensor'), may hold values from -0.15625 to 0.15625
- s_up: bfloat16 [1536, 1024], P('dp', 'tensor'), may hold values from -0.15625 to 0.15625
- s_down: bfloat16 [1024, 1536], P('tensor', 'dp'), may hold values from -0.25 to 0.25
Outputs:
- out_tokens: bfloat16 [2, 256, 128, 1536], P(None, 'tensor', 'dp')
- grad_tokens: bfloat16 [2, 256, 128, 1536], P(None, 'tensor', 'dp')
- grad_gain_attn: float32 [1536], replicated
- grad_gain_ffn: float32 [1536], replicated
- grad_query: float32 [1536, 1536], P('dp', 'tensor')
- grad_key: float32 [1536, 512], P('dp', 'tensor')
- grad_value: float32 [1536, 512], P('dp', 'tensor')
- grad_out: float32 [1536, 1536], P('tensor', 'dp')
- grad_router: float32 [1536, 8], replicated
- grad_gate: float32 [8, 1536, 512], P(None, 'dp', 'tensor')
- grad_up: float32 [8, 1536, 512], P(None, 'dp', 'tensor')
- grad_down: float32 [8, 512, 1536], P(None, 'tensor', 'dp')
- grad_sgate: float32 [1536, 1024], P('dp', 'tensor')
- grad_sup: float32 [1536, 1024], P('dp', 'tensor')
- grad_sdown: float32 [1024, 1536], P('tensor', 'dp')
The draws below stay inside these ranges and needn't reach their ends.
Inputs may be any that keep to these rules, and one draw needn't show every extreme that they name: For each micro-batch m and half t, perm[m, t, :] names each of 0 .. 127 once. A token's 6 routes name different experts. The lengths of one micro-batch add up to 24576, and the longest equals 128.
All inputs are finite; a program needn't handle non-finite values.
Results may differ from the reference program's by a relative error of at most 0.02.
Values may be sent and summed in bfloat16 or wider, within the bound.
No kernel may reach another device: no remote copies, remote signals or barrier semaphores. Data moves between devices by JAX's collectives and lax.ppermute only.
A program may use at most 320 MiB of HBM per device.

```python
import math
import jax
import jax.numpy as jnp
import numpy as np
from jax import lax

MODEL_WIDTH = 1536
QUERY_HEAD_COUNT = 12
KEY_VALUE_HEADS = 4
HEAD_SIZE = 128
FF = 512
FS = 1024
TOP = 6
EXPERTS = 8
CAP = 128
MB = 2
LONGEST_LENGTH = 128
SEQS_MB = 256
N_DP = 128
N_TENSOR = 2


def levels(rng, shape, split, smallest, high):
    loudness = 1.0
    for axis_at, parts in split:
        draws = jax.random.uniform(jax.random.fold_in(jax.random.fold_in(rng, 6), axis_at), (parts,), jnp.float32, smallest / len(split), high / len(split))
        loudness = loudness * jnp.repeat(jnp.exp(draws), shape[axis_at] // parts).reshape((-1,) + (1,) * (len(shape) - 1 - axis_at))
    return loudness


def different_ones(key, rows, count, top, lift):
    sequence = jax.random.permutation(jax.random.fold_in(key, 1), count)
    boost = sequence
    for power in range(3):
        boost = boost * boost // count
    boost = boost * lift // count
    chance = jax.random.randint(jax.random.fold_in(key, 2), (rows, count), 0, 4096) + boost
    sure = jax.random.permutation(jax.random.fold_in(key, 3), rows)[jnp.arange(count) % rows]
    chance = jnp.where(jnp.arange(rows)[:, None] == sure[None, :], 1 << 14, chance)
    priority = chance * count + jnp.arange(count)
    return lax.top_k(priority.astype(jnp.int32), top)[1].astype(jnp.int32)


def profile(amount, total, reach, skew):
    weights = [(1 << 20) // math.isqrt(grade ** skew) + 1 for grade in range(2, amount + 1)]
    spare, counts = total - reach - (amount - 1), [1] * (amount - 1)
    while spare > 0:
        movable = [i for i in range(amount - 1) if counts[i] < reach]
        whole, budget = sum([weights[i] for i in movable]), spare
        for i in movable:
            more = min(reach - counts[i], max(1, budget * weights[i] // whole), spare)
            counts[i] = counts[i] + more
            spare = spare - more
    return np.array([reach] + counts)


def uneven_parts(rng, count, total, most, lean):
    if count == 2:
        one = jax.random.randint(rng, (), max(1, total - most), min(most, total - 1) + 1)
        return jnp.stack([one, total - one])
    tallies = jnp.asarray(profile(count, total, most, lean), jnp.int32)
    pairs = (count - 1) // 2
    giver, sink = tallies[1:1 + 2 * pairs:2], tallies[2:2 + 2 * pairs:2]
    room = jnp.minimum(giver - 1, most - sink)
    passed = jax.random.randint(jax.random.fold_in(rng, 1), (pairs,), 0, 1 << 20) % (room + 1)
    tallies = tallies.at[1:1 + 2 * pairs:2].set(giver - passed).at[2:2 + 2 * pairs:2].set(sink + passed)
    return tallies[jax.random.permutation(jax.random.fold_in(rng, 2), count)]


def bell_draw(rng, extent, deviation, most, pieces=(), kind=jnp.bfloat16):
    level = levels(rng, extent, pieces, -0.22, 0.18) if pieces else 1.0
    values = jax.random.normal(rng, extent, jnp.float32) * deviation * level
    return jnp.minimum(jnp.maximum(values, -most), most).astype(kind)


def setup_inputs(seed: int = 0) -> dict:
    key_list = jax.random.split(jax.random.key(seed), 19)
    return {
        "tokens": bell_draw(key_list[0], (MB, SEQS_MB, LONGEST_LENGTH, MODEL_WIDTH), 1.0, 6.0, ((1, 2), (2, 128))),
        "cotangent": bell_draw(key_list[1], (MB, SEQS_MB, LONGEST_LENGTH, MODEL_WIDTH), 1.0, 6.0, ((1, 2), (2, 128))),
        "lengths": jax.vmap(lambda own: uneven_parts(own, SEQS_MB, SEQS_MB * LONGEST_LENGTH * 3 // 4, LONGEST_LENGTH, 2))(jax.random.split(key_list[2], MB)).reshape((MB, SEQS_MB)).astype(jnp.int32),
        "perm": jax.vmap(lambda own: jax.random.permutation(own, N_DP))(jax.random.split(key_list[3], MB * N_TENSOR)).reshape((MB, N_TENSOR, N_DP)).astype(jnp.int32),
        "routes": different_ones(key_list[4], MB * SEQS_MB * LONGEST_LENGTH, EXPERTS, TOP, 6144).reshape((MB, SEQS_MB, LONGEST_LENGTH, TOP)),
        "gain_attn": jnp.clip(1.0 + 0.1 * jax.random.normal(key_list[5], (MODEL_WIDTH,), jnp.float32), 0.5, 1.5),
        "gain_ffn": jnp.clip(1.0 + 0.1 * jax.random.normal(key_list[6], (MODEL_WIDTH,), jnp.float32), 0.5, 1.5),
        "query_matrix": bell_draw(key_list[7], (MODEL_WIDTH, QUERY_HEAD_COUNT * HEAD_SIZE), MODEL_WIDTH ** -0.5, 0.15625, ((0, 128), (1, 2))),
        "key_matrix": bell_draw(key_list[8], (MODEL_WIDTH, KEY_VALUE_HEADS * HEAD_SIZE), MODEL_WIDTH ** -0.5, 0.15625, ((0, 128), (1, 2))),
        "value_matrix": bell_draw(key_list[9], (MODEL_WIDTH, KEY_VALUE_HEADS * HEAD_SIZE), MODEL_WIDTH ** -0.5, 0.15625, ((0, 128), (1, 2))),
        "w_out": bell_draw(key_list[10], (QUERY_HEAD_COUNT * HEAD_SIZE, MODEL_WIDTH), (QUERY_HEAD_COUNT * HEAD_SIZE * 4 // LONGEST_LENGTH) ** -0.5, 0.875, ((0, 2), (1, 128))),
        "w_router": bell_draw(key_list[11], (MODEL_WIDTH, EXPERTS), (4 * MODEL_WIDTH) ** -0.5, 0.078125),
        "w_gate": bell_draw(key_list[12], (EXPERTS, MODEL_WIDTH, FF), MODEL_WIDTH ** -0.5, 0.15625, ((1, 128), (2, 2))),
        "w_up": bell_draw(key_list[13], (EXPERTS, MODEL_WIDTH, FF), MODEL_WIDTH ** -0.5, 0.15625, ((1, 128), (2, 2))),
        "w_down": bell_draw(key_list[14], (EXPERTS, FF, MODEL_WIDTH), (FF // 8) ** -0.5, 0.75, ((1, 2), (2, 128))),
        "s_gate": bell_draw(key_list[15], (MODEL_WIDTH, FS), MODEL_WIDTH ** -0.5, 0.15625, ((0, 128), (1, 2))),
        "s_up": bell_draw(key_list[16], (MODEL_WIDTH, FS), MODEL_WIDTH ** -0.5, 0.15625, ((0, 128), (1, 2))),
        "s_down": bell_draw(key_list[17], (FS, MODEL_WIDTH), (FS // 2) ** -0.5, 0.25, ((0, 2), (1, 128))),
    }


EPS = 1e-06
HIGH = lax.Precision.HIGHEST

@jax.custom_vjp
def low(v):
    return lax.optimization_barrier(v.astype(jnp.bfloat16)).astype(jnp.float32)

@jax.custom_vjp
def low_back(v):
    return v

def low_keep(v):
    return (low(v), None)

def low_pass(kept, grad):
    return (grad,)

def back_keep(v):
    return (v, None)

def back_low(kept, grad):
    return (low(grad),)
low.defvjp(low_keep, low_pass)
low_back.defvjp(back_keep, back_low)

def matrix_product(left, right):
    return jnp.dot(left, right, precision=HIGH, preferred_element_type=jnp.float32)

def normalize(value_rows, gain):
    return value_rows * lax.rsqrt(lax.optimization_barrier(jnp.mean(value_rows * value_rows, axis=-1, keepdims=True)) + EPS) * gain

def slot_plan(route_rows, valid):
    experts_iota = jnp.arange(EXPERTS, dtype=jnp.int32)
    named = lax.optimization_barrier(jnp.sum((route_rows[:, :, None] == experts_iota[None, None, :]).astype(jnp.int32), axis=1)).astype(jnp.int32)
    hits = (named * valid[:, None].astype(jnp.int32)).astype(jnp.int32)
    before = (jnp.cumsum(hits, axis=0).astype(jnp.int32) - hits).astype(jnp.int32)
    ranked = jnp.take_along_axis(before, route_rows, axis=1).astype(jnp.int32)
    kept = jnp.logical_and(valid[:, None], ranked < CAP)
    target = jnp.where(kept, route_rows * CAP + ranked, -1).astype(jnp.int32)
    return (kept, target)

def run_block(x, route_rows, valid, weights):
    gain_attn, gain_ffn, query_matrix, key_matrix, value_matrix, w_out, w_router, w_gate, w_up, w_down, s_gate, s_up, s_down = weights
    rows = x.shape[0]
    block_list = rows // LONGEST_LENGTH
    head_group = QUERY_HEAD_COUNT // KEY_VALUE_HEADS
    normed_input = low(normalize(x, gain_attn))
    query_rows = low(low_back(matrix_product(normed_input, query_matrix))).reshape(block_list, LONGEST_LENGTH, KEY_VALUE_HEADS, head_group, HEAD_SIZE)
    key = low(low_back(matrix_product(normed_input, key_matrix))).reshape(block_list, LONGEST_LENGTH, KEY_VALUE_HEADS, HEAD_SIZE)
    value_rows = low(low_back(matrix_product(normed_input, value_matrix))).reshape(block_list, LONGEST_LENGTH, KEY_VALUE_HEADS, HEAD_SIZE)
    scores = low_back(jnp.einsum('slkgd,smkd->skglm', query_rows, key, precision=HIGH) * (1.0 / math.sqrt(HEAD_SIZE)))
    place = jnp.arange(LONGEST_LENGTH, dtype=jnp.int32)
    scores = jnp.where(place[None, :] <= place[:, None], scores, -1e+30)
    probs = jax.nn.softmax(scores, axis=-1)
    mixed = jnp.einsum('skglm,smkd->slkgd', low(probs), value_rows, precision=HIGH)
    mixed = low(low_back(mixed)).reshape(rows, QUERY_HEAD_COUNT * HEAD_SIZE)
    hidden = x + low_back(matrix_product(mixed, w_out))
    normed_ffn = low(normalize(hidden, gain_ffn))
    logits = matrix_product(normed_ffn, w_router)
    gates = jax.nn.softmax(jnp.take_along_axis(logits, route_rows, axis=1), axis=-1)
    kept, target = slot_plan(route_rows, valid)
    slot_iota = jnp.arange(EXPERTS * CAP, dtype=jnp.int32)
    table = lax.optimization_barrier(jnp.sum((slot_iota[:, None, None] == target[None, :, :]).astype(jnp.float32), axis=2))
    expert_in = matrix_product(table, normed_ffn).reshape(EXPERTS, CAP, MODEL_WIDTH)
    gate_act = low_back(jnp.einsum('ecd,edf->ecf', expert_in, w_gate, precision=HIGH))
    up_act = low_back(jnp.einsum('ecd,edf->ecf', expert_in, w_up, precision=HIGH))
    inner = low(jax.nn.silu(gate_act) * up_act)
    expert_out = low_back(jnp.einsum('ecf,efd->ecd', inner, w_down, precision=HIGH)).reshape(EXPERTS * CAP, MODEL_WIDTH)
    kept_gates = jnp.where(kept, gates, 0.0)
    routed = lax.optimization_barrier(jnp.sum(kept_gates[:, :, None] * jnp.take(expert_out, jnp.maximum(target, 0), axis=0), axis=1))
    shared_gate = low_back(matrix_product(normed_ffn, s_gate))
    shared_up = low_back(matrix_product(normed_ffn, s_up))
    shared_inner = low(jax.nn.silu(shared_gate) * shared_up)
    shared_out = low_back(matrix_product(shared_inner, s_down))
    return jnp.where(valid[:, None], hidden + routed + shared_out, 0.0)

def run_layer(floats, routes, lengths, perm):
    tokens = floats[0]
    weights = floats[1:]
    batches = tokens.shape[0]
    offsets = jnp.arange(N_TENSOR, dtype=jnp.int32)[None, :, None] * N_DP
    dealt = jnp.transpose(perm + offsets, (0, 2, 1)).reshape(batches, N_DP * N_TENSOR).astype(jnp.int32)

    def select_rows(block, index):
        return jnp.take(block, index, axis=0)
    count = batches * N_DP
    x_blocks = jax.vmap(select_rows)(tokens, dealt).reshape(count, N_TENSOR * LONGEST_LENGTH, MODEL_WIDTH)
    route_blocks = jax.vmap(select_rows)(routes, dealt).reshape(count, N_TENSOR * LONGEST_LENGTH, TOP)
    length_blocks = jax.vmap(select_rows)(lengths, dealt).reshape(count, N_TENSOR)
    place = jnp.arange(LONGEST_LENGTH, dtype=jnp.int32)
    valid = (place[None, None, :] < length_blocks[:, :, None]).reshape(count, N_TENSOR * LONGEST_LENGTH)
    head_group = math.gcd(count, max(1, 4096 // (N_TENSOR * LONGEST_LENGTH)))
    steps_count = count // head_group
    x_groups = x_blocks.reshape(steps_count, head_group, N_TENSOR * LONGEST_LENGTH, MODEL_WIDTH)
    route_groups = route_blocks.reshape(steps_count, head_group, N_TENSOR * LONGEST_LENGTH, TOP)
    valid_groups = valid.reshape(steps_count, head_group, N_TENSOR * LONGEST_LENGTH)

    def one_group(inputs):
        return jax.vmap(lambda a, b, c: run_block(a, b, c, weights))(*inputs)
    checked = jax.checkpoint(one_group)

    def scan_step(carry, inputs):
        return (carry, checked(inputs))
    start = jnp.zeros((), jnp.float32)
    unused, outs = lax.scan(scan_step, start, (x_groups, route_groups, valid_groups))
    out_blocks = outs.reshape(batches, N_DP * N_TENSOR, LONGEST_LENGTH, MODEL_WIDTH)

    def place_back(block, index):
        return jnp.zeros_like(block).at[index].set(block)
    return jax.vmap(place_back)(out_blocks, dealt)

def reference(tokens, cotangent, lengths, perm, routes, gain_attn, gain_ffn, query_matrix, key_matrix, value_matrix, w_out, w_router, w_gate, w_up, w_down, s_gate, s_up, s_down):
    floats = tuple((item.astype(jnp.float32) for item in (tokens, gain_attn, gain_ffn, query_matrix, key_matrix, value_matrix, w_out, w_router, w_gate, w_up, w_down, s_gate, s_up, s_down)))

    def forward(*values):
        return run_layer(values, routes, lengths, perm)
    result, pull = jax.vjp(forward, *floats)
    grads = pull(cotangent.astype(jnp.float32))
    return (result.astype(jnp.bfloat16), grads[0].astype(jnp.bfloat16), grads[1], grads[2], grads[3], grads[4], grads[5], grads[6], grads[7], grads[8], grads[9], grads[10], grads[11], grads[12], grads[13])
```

```python
import math

import jax
import jax.numpy as jnp
import numpy as np
from jax import lax
from jax.sharding import Mesh
from jax.sharding import PartitionSpec as P

QUERY_HEAD_COUNT = 12
KEY_VALUE_HEADS = 4
HEAD_SIZE = 128
GROUP = QUERY_HEAD_COUNT // KEY_VALUE_HEADS
CAP = 128
EPS = 1e-06
DP = ("x", "zl", "y", "c")
EVERY = ("x", "zl", "y", "c", "zh")
SWAP = ((0, 1), (1, 0))
F32 = jnp.float32
BF16 = jnp.bfloat16


def dot(left, right, contract, out=F32):
    result = lax.dot_general(
        left, right, (((contract[0],), (contract[1],)), ((), ())), preferred_element_type=F32
    )
    return result.astype(out)


def swapped(value, axis):
    return lax.ppermute(value, axis, SWAP)


def whole_rows(own):
    pair = jnp.concatenate([own, swapped(own, "zh")], axis=0)
    return jnp.concatenate([pair, swapped(pair, "c")], axis=0)


def rows_back(part):
    half = part.shape[0] // 2
    both = part[:half].astype(F32) + swapped(part[half:], "c").astype(F32)
    quarter = half // 2
    sent = swapped(both[quarter:].astype(BF16), "zh")
    return both[:quarter] + sent.astype(F32)


def gathered(shard):
    near = lax.all_gather(shard, "zl", axis=0, tiled=True)
    return lax.all_gather(near, ("x", "y"), axis=0, tiled=True)


def scattered(total):
    near = lax.psum_scatter(total, ("x", "y"), scatter_dimension=0, tiled=True)
    return lax.psum_scatter(near, "zl", scatter_dimension=0, tiled=True)


def silu_slope(value):
    sigma = jax.nn.sigmoid(value)
    return sigma * (1.0 + value * (1.0 - sigma))


def attention_scores(query, key):
    scaled = jnp.einsum("slgd,smd->sglm", query, key, preferred_element_type=F32) * (
        1.0 / math.sqrt(HEAD_SIZE)
    )
    place = jnp.arange(query.shape[1], dtype=jnp.int32)
    return jnp.where(place[None, :] <= place[:, None], scaled, -1e30)


def on_device(
    tokens,
    cotangent,
    lengths,
    perm,
    routes,
    gain_attn,
    gain_ffn,
    query_matrix,
    key_matrix,
    value_matrix,
    w_out,
    w_router,
    w_gate,
    w_up,
    w_down,
    s_gate,
    s_up,
    s_down,
):
    t = lax.axis_index("zh")
    place_here = lax.axis_index(DP)
    side_x, side_zl, side_y = (lax.axis_size(a) for a in ("x", "zl", "y"))
    batches, seqs = tokens.shape[0], tokens.shape[1]
    seq_len = lax.axis_size(DP)
    width = tokens.shape[3]
    experts = w_gate.shape[0]
    rows_here = query_matrix.shape[0]

    def halves(value):
        return jnp.moveaxis(value.reshape(*value.shape[:-1], 2, value.shape[-1] // 2), -2, 0)

    def expert_halves(value):
        both = value.reshape(experts, rows_here, 2, value.shape[-1] // 2)
        return jnp.transpose(both, (2, 1, 0, 3)).reshape(2, rows_here, -1)

    attn_shard = jnp.concatenate(
        [halves(query_matrix), halves(key_matrix), halves(value_matrix), halves(w_out.T)], axis=2
    )
    ffn_shard = jnp.concatenate(
        [
            expert_halves(w_gate),
            halves(s_gate),
            expert_halves(w_up),
            halves(s_up),
            expert_halves(jnp.swapaxes(w_down, 1, 2)),
            halves(s_down.T),
        ],
        axis=2,
    )
    attn_cols = attn_shard.shape[2]
    both_shards = jnp.concatenate([attn_shard, ffn_shard], axis=2)
    chip_rows = lax.all_to_all(both_shards, "c", 0, 0, tiled=True)
    chip_rows = chip_rows.reshape(2 * rows_here, -1)
    attn_w = gathered(chip_rows[:, :attn_cols])
    ffn_w = gathered(chip_rows[:, attn_cols:])
    q_cols = query_matrix.shape[1] // 2
    k_cols = key_matrix.shape[1] // 2
    qkv_cols = q_cols + 2 * k_cols
    qkv_w, out_w = attn_w[:, :qkv_cols], attn_w[:, qkv_cols:]
    hidden_e = w_gate.shape[2] // 2
    hidden = experts * hidden_e + s_gate.shape[1] // 2
    up_w, down_w = ffn_w[:, : 2 * hidden], ffn_w[:, 2 * hidden :]

    def reorder(value):
        parts = value.reshape(side_x, side_zl, side_y, -1, *value.shape[1:])
        return jnp.swapaxes(parts, 1, 2).reshape(value.shape)

    unit = width // (side_x * side_zl * side_y)
    iota = jnp.arange(width, dtype=jnp.int32)
    mate = (
        (iota // (unit * side_y * side_zl)) * (unit * side_y * side_zl)
        + ((iota // unit) % side_zl) * (unit * side_y)
        + ((iota // (unit * side_zl)) % side_y) * unit
        + iota % unit
    )
    features = (iota[:, None] == mate[None, :]).astype(BF16)
    order = lax.dynamic_index_in_dim(perm, t, 1, False)
    deal = (order[:, :, None] == jnp.arange(seqs, dtype=jnp.int32)[None, None, :]).astype(BF16)
    own_routes = lax.dynamic_slice_in_dim(routes[:, :, 0], t * seqs, seqs, 1)
    own_lengths = lax.dynamic_slice_in_dim(lengths, t * seqs, seqs, 1)
    own_valid = place_here < own_lengths
    named = jnp.any(
        own_routes[:, :, :, None] == jnp.arange(experts, dtype=jnp.int32), axis=2
    )
    marks = jnp.concatenate(
        [jnp.logical_and(named, own_valid[:, :, None]), own_valid[:, :, None]], axis=2
    ).astype(BF16)
    marks = jnp.pad(marks, ((0, 0), (0, 0), (0, 128 - marks.shape[2])))

    def dealt(value):
        sent = jnp.einsum("mjs,msd->jmd", deal, value, preferred_element_type=F32)
        sent = sent.astype(BF16).reshape(seqs, -1, 128)
        got = lax.all_to_all(sent, DP, 0, 0, tiled=True)
        got = jnp.swapaxes(got.reshape(seq_len, batches, -1), 0, 1)
        return got.reshape(batches * seq_len, -1)

    own_in = dealt(jnp.concatenate([tokens[:, :, 0], marks], axis=2))
    own_marks = own_in[:, width:]
    x_own = dot(own_in[:, :width], features, (1, 0))
    own_cot = dealt(cotangent[:, :, 0])
    own_keep = own_marks[:, experts : experts + 1].astype(F32)
    gy_own = own_keep * dot(own_cot, features, (1, 0))

    gain_a, gain_f = reorder(gain_attn), reorder(gain_ffn)
    router = reorder(w_router)
    scale_attn = lax.rsqrt(jnp.mean(x_own * x_own, axis=-1, keepdims=True) + EPS)
    unit_attn = x_own * scale_attn
    both = whole_rows(
        jnp.concatenate([(unit_attn * gain_a).astype(BF16), own_marks], axis=1)
    )
    n1, marks_all = both[:, :width], both[:, width:]
    gy = whole_rows(gy_own.astype(BF16))
    rows = n1.shape[0]
    count = rows // seq_len
    qkv = dot(n1, qkv_w, (1, 0), BF16)
    query = qkv[:, :q_cols].reshape(count, seq_len, GROUP, HEAD_SIZE)
    key = qkv[:, q_cols : q_cols + k_cols].reshape(count, seq_len, HEAD_SIZE)
    value = qkv[:, q_cols + k_cols :].reshape(count, seq_len, HEAD_SIZE)
    scores = attention_scores(query, key)
    log_total = jax.nn.logsumexp(scores, axis=-1, keepdims=True)
    probs = jnp.exp(scores - log_total)
    probs_low = probs.astype(BF16)
    mixed = jnp.einsum("sglm,smd->slgd", probs_low, value, preferred_element_type=F32)
    mixed = mixed.astype(BF16).reshape(rows, q_cols)
    h_own = x_own + rows_back(dot(mixed, out_w, (1, 1), BF16))

    scale_ffn = lax.rsqrt(jnp.mean(h_own * h_own, axis=-1, keepdims=True) + EPS)
    unit_ffn = h_own * scale_ffn
    n2 = whole_rows((unit_ffn * gain_f).astype(BF16))
    logits = dot(n2, router, (1, 0))
    hits = marks_all[:, :experts]
    per_seq = hits.reshape(2, 2, batches, seq_len, experts)
    place = jnp.arange(seq_len, dtype=jnp.int32)
    earlier = (place[None, :] < place[:, None]).astype(BF16)
    before = jnp.einsum("pq,ctmqe->ctmpe", earlier, per_seq, preferred_element_type=F32)
    totals = jnp.sum(per_seq.astype(F32), axis=3, keepdims=True)
    is_later = jnp.stack([t == 1, t == 0]).astype(F32)[None, :, None, None, None]
    rank = before + is_later * totals[:, ::-1]
    named_all = hits > 0
    kept = jnp.logical_and(named_all, rank.reshape(rows, experts) < CAP)
    top = jnp.max(jnp.where(named_all, logits, -1e30), axis=1, keepdims=True)
    powers = jnp.where(named_all, jnp.exp(jnp.where(named_all, logits - top, 0.0)), 0.0)
    gates = powers / jnp.maximum(jnp.sum(powers, axis=1, keepdims=True), 1e-30)
    kept_gates = jnp.where(kept, gates, 0.0)

    def spread(per_expert):
        wide = jnp.broadcast_to(per_expert[:, :, None], (rows, experts, hidden_e))
        return jnp.concatenate(
            [wide.reshape(rows, -1), jnp.ones((rows, hidden - experts * hidden_e), F32)], axis=1
        )

    weight = spread(kept_gates)
    ab = dot(n2, up_w, (1, 0))
    a, b = ab[:, :hidden], ab[:, hidden:]
    silu_a = jax.nn.silu(a)
    inner = (silu_a * b).astype(BF16)
    weighted = (weight * inner.astype(F32)).astype(BF16)
    branch = rows_back(dot(weighted, down_w, (1, 1), BF16))
    out_own = (own_keep * (h_own + branch)).astype(BF16)

    dhid = dot(gy, down_w, (1, 0))
    dgates = jnp.sum(
        (inner.astype(F32) * dhid)[:, : experts * hidden_e].reshape(rows, experts, hidden_e), axis=2
    )
    dgates = jnp.where(kept, dgates, 0.0)
    dlogits = gates * (dgates - jnp.sum(gates * dgates, axis=1, keepdims=True))
    dinner = weight * dhid
    dab = jnp.concatenate(
        [(dinner * b * silu_slope(a)).astype(BF16), (dinner * silu_a).astype(BF16)], axis=1
    )
    dn2_part = dot(dab, up_w, (1, 1)) + dot(dlogits.astype(BF16), router, (1, 1))
    dn2 = rows_back(dn2_part.astype(BF16))
    big_ffn = jnp.concatenate(
        [dot(n2, dab, (0, 0), BF16), dot(gy, weighted, (0, 0), BF16)], axis=1
    )
    dn2, big_ffn = lax.optimization_barrier((dn2, big_ffn))
    grad_ffn_w = scattered(big_ffn)
    small_router = dot(n2, dlogits.astype(BF16), (0, 0))
    small_ffn = jnp.sum(dn2 * unit_ffn, axis=0)
    scaled = dn2 * gain_f
    dh = gy_own + scale_ffn * (
        scaled - unit_ffn * jnp.mean(scaled * unit_ffn, axis=-1, keepdims=True)
    )

    dattn = whole_rows(dh.astype(BF16))
    dmixed = dot(dattn, out_w, (1, 0), BF16)
    big_out = dot(dattn, mixed, (0, 0), BF16)
    dheads = dmixed.reshape(count, seq_len, GROUP, HEAD_SIZE)
    dprobs = jnp.einsum("slgd,smd->sglm", dheads, value, preferred_element_type=F32)
    dscores = (probs * (dprobs - jnp.sum(probs * dprobs, axis=-1, keepdims=True))).astype(BF16)
    root = 1.0 / math.sqrt(HEAD_SIZE)
    dq = jnp.einsum("sglm,smd->slgd", dscores, key, preferred_element_type=F32) * root
    dk = jnp.einsum("sglm,slgd->smd", dscores, query, preferred_element_type=F32) * root
    dv = jnp.einsum("sglm,slgd->smd", probs_low, dheads, preferred_element_type=F32)
    dqkv = jnp.concatenate(
        [
            dq.astype(BF16).reshape(rows, -1),
            dk.astype(BF16).reshape(rows, -1),
            dv.astype(BF16).reshape(rows, -1),
        ],
        axis=1,
    )
    dn1 = rows_back(dot(dqkv, qkv_w, (1, 1), BF16))
    big_attn = jnp.concatenate([dot(n1, dqkv, (0, 0), BF16), big_out], axis=1)
    grad_attn_w = scattered(big_attn)
    small_attn = jnp.sum(dn1 * unit_attn, axis=0)
    scaled = dn1 * gain_a
    dx_own = dh + scale_attn * (
        scaled - unit_attn * jnp.mean(scaled * unit_attn, axis=-1, keepdims=True)
    )
    dx_own = dx_own.astype(BF16)

    def returned(own):
        natural = dot(own, features, (1, 0), BF16).reshape(batches, seq_len, -1)
        sent = jnp.swapaxes(natural, 0, 1).reshape(seq_len, -1, 128)
        got = lax.all_to_all(sent, DP, 0, 0, tiled=True).reshape(seqs, batches, -1)
        back = jnp.einsum("mjs,jmd->msd", deal, got, preferred_element_type=F32)
        return back.astype(BF16)[:, :, None]

    out_tokens = returned(out_own)
    grad_tokens = returned(dx_own)

    small = jnp.concatenate([small_attn[None], small_ffn[None], small_router.T], axis=0)
    small = lax.psum(small, EVERY)
    final = reorder(small.T)

    mine = jnp.concatenate([grad_attn_w, grad_ffn_w], axis=1).reshape(2, rows_here, -1)
    mine = lax.all_to_all(mine, "c", 0, 0, tiled=True).astype(F32)

    def join(start, cols):
        part = mine[:, :, start : start + cols]
        return jnp.swapaxes(part, 0, 1).reshape(rows_here, 2 * cols)

    def join_experts(start):
        part = mine[:, :, start : start + experts * hidden_e]
        part = part.reshape(2, rows_here, experts, hidden_e)
        return jnp.transpose(part, (2, 1, 0, 3)).reshape(experts, rows_here, 2 * hidden_e)

    shared_cols = s_gate.shape[1] // 2
    ffn_at = attn_cols
    each = experts * hidden_e
    return (
        out_tokens,
        grad_tokens,
        final[:, 0],
        final[:, 1],
        join(0, q_cols),
        join(q_cols, k_cols),
        join(q_cols + k_cols, k_cols),
        join(qkv_cols, q_cols).T,
        final[:, 2:],
        join_experts(ffn_at),
        join_experts(ffn_at + hidden),
        jnp.swapaxes(join_experts(ffn_at + 2 * hidden), 1, 2),
        join(ffn_at + each, shared_cols),
        join(ffn_at + hidden + each, shared_cols),
        join(ffn_at + 2 * hidden + each, shared_cols).T,
    )


def solution(mesh):
    devices = np.asarray(mesh.devices)
    side = round((devices.shape[0] // 2) ** (1 / 3))
    fine = Mesh(devices.reshape(side, side, side, 2, 2), EVERY)
    rows, cols = P(DP, "zh"), P("zh", DP)
    seqs = P(None, "zh", DP, None)
    return jax.shard_map(
        on_device,
        mesh=fine,
        in_specs=(
            seqs,
            seqs,
            P(),
            P(),
            P(None, None, DP, None),
            P(),
            P(),
            rows,
            rows,
            rows,
            cols,
            P(),
            P(None, DP, "zh"),
            P(None, DP, "zh"),
            P(None, "zh", DP),
            rows,
            rows,
            cols,
        ),
        out_specs=(
            seqs,
            seqs,
            P(),
            P(),
            rows,
            rows,
            rows,
            cols,
            P(),
            P(None, DP, "zh"),
            P(None, DP, "zh"),
            P(None, "zh", DP),
            rows,
            rows,
            cols,
        ),
        check_vma=False,
    )
```

```python
import math

import jax
import jax.numpy as jnp
import numpy as np
from jax import lax
from jax.sharding import Mesh
from jax.sharding import PartitionSpec as P

QUERY_HEAD_COUNT = 12
KEY_VALUE_HEADS = 4
HEAD_SIZE = 128
GROUP = QUERY_HEAD_COUNT // KEY_VALUE_HEADS
CAP = 128
EPS = 1e-06
DP = ("x", "z1", "z0", "y", "c")
EVERY = ("x", "z1", "z0", "y", "c", "zh")
F32 = jnp.float32
BF16 = jnp.bfloat16


def dot(left, right, contract, out=F32):
    result = lax.dot_general(
        left, right, (((contract[0],), (contract[1],)), ((), ())), preferred_element_type=F32
    )
    return result.astype(out)


def swapped(value, axis, bit=1):
    return lax.ppermute(value, axis, [(i, i ^ bit) for i in range(lax.axis_size(axis))])


def whole_rows(own):
    pair = jnp.concatenate([own, swapped(own, "z0")], axis=0)
    return jnp.concatenate([pair, swapped(pair, "c")], axis=0)


def rows_back(part):
    half = part.shape[0] // 2
    both = part[:half].astype(F32) + swapped(part[half:], "c").astype(F32)
    quarter = half // 2
    sent = swapped(both[quarter:].astype(BF16), "z0")
    return both[:quarter] + sent.astype(F32)


def z_routes():
    wide = lax.axis_size("z1")
    found = []
    for k1 in range(wide):
        for k2 in range(2):
            pairs = []
            for z1 in range(wide):
                for z0 in range(2):
                    for zh in range(2):
                        goal = ((z1 ^ k1) * 2 + zh) * 2 + (z0 ^ k2)
                        pairs.append(((z1 * 2 + z0) * 2 + zh, goal))
            found.append(pairs)
    return found


def z_gathered(shard):
    return jnp.concatenate(
        [lax.ppermute(shard, ("z1", "z0", "zh"), pairs) for pairs in z_routes()], axis=0
    )


def z_scattered(near):
    routes = z_routes()
    pieces = near.reshape(len(routes), -1, near.shape[1])
    total = 0.0
    for piece, pairs in zip(pieces, routes):
        back = [(goal, start) for start, goal in pairs]
        total = total + lax.ppermute(piece, ("z1", "z0", "zh"), back).astype(F32)
    return total.astype(BF16)


def xy_gathered(near):
    return lax.all_gather(near, ("x", "y"), axis=0, tiled=True)


def xy_scattered(total):
    return lax.psum_scatter(total, ("x", "y"), scatter_dimension=0, tiled=True)


def xy_scattered_apart(total):
    count = lax.axis_size(("x", "y"))
    pieces = total.reshape(count, -1, total.shape[1])
    got = lax.all_to_all(pieces, ("x", "y"), 0, 0, tiled=True)
    return jnp.sum(got.astype(F32), axis=0).astype(BF16)


def summed_everywhere(value):
    for axis in EVERY:
        bit = 1
        while bit < lax.axis_size(axis):
            value = value + swapped(value, axis, bit)
            bit *= 2
    return value


def silu_slope(value):
    sigma = jax.nn.sigmoid(value)
    return sigma * (1.0 + value * (1.0 - sigma))


def attention_scores(query, key):
    scaled = jnp.einsum("slgd,smd->sglm", query, key, preferred_element_type=F32) * (
        1.0 / math.sqrt(HEAD_SIZE)
    )
    place = jnp.arange(query.shape[1], dtype=jnp.int32)
    return jnp.where(place[None, :] <= place[:, None], scaled, -1e30)


def on_device(
    tokens,
    cotangent,
    lengths,
    perm,
    routes,
    gain_attn,
    gain_ffn,
    query_matrix,
    key_matrix,
    value_matrix,
    w_out,
    w_router,
    w_gate,
    w_up,
    w_down,
    s_gate,
    s_up,
    s_down,
):
    t = lax.axis_index("zh")
    place_here = lax.axis_index(DP)
    side_x, side_z1, side_z0, side_y = (lax.axis_size(a) for a in ("x", "z1", "z0", "y"))
    side_zl = side_z1 * side_z0
    flips = (lax.axis_index("z1"), t)
    batches, seqs = tokens.shape[0], tokens.shape[1]
    seq_len = lax.axis_size(DP)
    width = tokens.shape[3]
    experts = w_gate.shape[0]
    rows_here = query_matrix.shape[0]

    def halves(value):
        cols = value.shape[-1] // 2
        return value[..., :cols], value[..., cols:]

    def by_row(value):
        return jnp.concatenate([value[e] for e in range(experts)], axis=1)

    attn_parts = [halves(v) for v in (query_matrix, key_matrix, value_matrix, w_out.T)]
    ffn_parts = [
        tuple(by_row(v) for v in halves(w_gate)),
        halves(s_gate),
        tuple(by_row(v) for v in halves(w_up)),
        halves(s_up),
        tuple(by_row(v) for v in halves(jnp.swapaxes(w_down, 1, 2))),
        halves(s_down.T),
    ]
    attn_cols = sum(p[0].shape[1] for p in attn_parts)
    both_shards = jnp.stack(
        [jnp.concatenate([p[c] for p in attn_parts + ffn_parts], axis=1) for c in (0, 1)]
    )
    chip_rows = lax.all_to_all(both_shards, "c", 0, 0, tiled=True)
    chip_rows = chip_rows.reshape(2 * rows_here, -1)
    near = z_gathered(chip_rows)
    attn_w = xy_gathered(near[:, :attn_cols])
    ffn_w = xy_gathered(near[:, attn_cols:])
    q_cols = query_matrix.shape[1] // 2
    k_cols = key_matrix.shape[1] // 2
    qkv_cols = q_cols + 2 * k_cols
    qkv_w, out_w = attn_w[:, :qkv_cols], attn_w[:, qkv_cols:]
    hidden_e = w_gate.shape[2] // 2
    hidden = experts * hidden_e + s_gate.shape[1] // 2
    up_w, down_w = ffn_w[:, : 2 * hidden], ffn_w[:, 2 * hidden :]

    def flipped(value, axes):
        for axis, flip in zip(axes, flips):
            value = jnp.where(flip == 1, jnp.flip(value, axis), value)
        return value

    def to_local(value):
        parts = value.reshape(-1, side_x, side_z1, side_z0, side_y, width // (seq_len // 2))
        return flipped(jnp.transpose(parts, (0, 1, 4, 2, 3, 5)), (3, 4)).reshape(value.shape)

    def to_natural(value):
        parts = value.reshape(-1, side_x, side_y, side_z1, side_z0, width // (seq_len // 2))
        return jnp.transpose(flipped(parts, (3, 4)), (0, 1, 3, 4, 2, 5)).reshape(value.shape)

    unit = width // (seq_len // 2)
    iota = jnp.arange(width, dtype=jnp.int32)
    piece = iota // unit
    zl_of = (piece % side_zl) ^ (flips[0] * 2 + flips[1])
    mate = (
        ((piece // (side_zl * side_y)) * side_zl + zl_of) * side_y + (piece // side_zl) % side_y
    ) * unit + iota % unit
    features = (iota[:, None] == mate[None, :]).astype(BF16)

    order = lax.dynamic_index_in_dim(perm, t, 1, False)
    deal = (order[:, :, None] == jnp.arange(seqs, dtype=jnp.int32)[None, None, :]).astype(BF16)
    own_routes = lax.dynamic_slice_in_dim(routes[:, :, 0], t * seqs, seqs, 1)
    own_lengths = lax.dynamic_slice_in_dim(lengths, t * seqs, seqs, 1)
    own_valid = place_here < own_lengths
    named = jnp.any(
        own_routes[:, :, :, None] == jnp.arange(experts, dtype=jnp.int32), axis=2
    )
    marks = jnp.concatenate(
        [jnp.logical_and(named, own_valid[:, :, None]), own_valid[:, :, None]], axis=2
    ).astype(BF16)
    marks = jnp.pad(marks, ((0, 0), (0, 0), (0, 128 - marks.shape[2])))
    rows_in = jnp.concatenate([tokens[:, :, 0], marks, cotangent[:, :, 0]], axis=2)
    sent = jnp.einsum("mjs,msd->jmd", deal, rows_in, preferred_element_type=F32)
    sent = sent.astype(BF16).reshape(seqs, -1, 128)
    got = lax.all_to_all(sent, DP, 0, 0, tiled=True).reshape(seq_len, batches, -1)
    own_in = jnp.swapaxes(got, 0, 1)
    x_own = dot(own_in[:, :, :width].reshape(batches * seq_len, width), features, (1, 0))
    own_marks = own_in[:, :, width : width + 128]
    own_hits = own_marks[:, :, :experts]
    own_keep = own_marks[:, :, experts].reshape(-1, 1).astype(F32)
    gy_own = own_keep * dot(
        own_in[:, :, width + 128 :].reshape(batches * seq_len, width), features, (1, 0)
    )

    place = jnp.arange(seq_len, dtype=jnp.int32)
    earlier = (place[None, :] < place[:, None]).astype(BF16)
    before = jnp.einsum("pq,mqe->mpe", earlier, own_hits, preferred_element_type=F32)
    totals = jnp.sum(own_hits.astype(F32), axis=1)
    other_totals = swapped(totals, "zh")
    rank = before + jnp.where(t == 1, other_totals, 0.0)[:, None, :]
    own_kept = jnp.where(rank < CAP, own_hits, jnp.zeros_like(own_hits))
    flags = jnp.concatenate([own_hits, own_kept], axis=2).reshape(batches * seq_len, -1)
    flags = jnp.pad(flags, ((0, 0), (0, 128 - flags.shape[1])))

    small_in = to_local(
        jnp.concatenate([gain_attn[None], gain_ffn[None], w_router.T.astype(F32)], axis=0)
    )
    gain_a, gain_f, router = small_in[0:1], small_in[1:2], small_in[2:].astype(BF16)
    scale_attn = lax.rsqrt(jnp.mean(x_own * x_own, axis=-1, keepdims=True) + EPS)
    unit_attn = x_own * scale_attn
    n1 = whole_rows((unit_attn * gain_a).astype(BF16))
    gy_own_low = jnp.concatenate([gy_own.astype(BF16), flags], axis=1)
    n1, gy_own_low = lax.optimization_barrier((n1, gy_own_low))
    both = whole_rows(gy_own_low)
    gy, flags_all = both[:, :width], both[:, width:]
    rows = n1.shape[0]
    count = rows // seq_len
    qkv = dot(n1, qkv_w, (1, 0), BF16)
    query = qkv[:, :q_cols].reshape(count, seq_len, GROUP, HEAD_SIZE)
    key = qkv[:, q_cols : q_cols + k_cols].reshape(count, seq_len, HEAD_SIZE)
    value = qkv[:, q_cols + k_cols :].reshape(count, seq_len, HEAD_SIZE)
    scores = attention_scores(query, key)
    log_total = jax.nn.logsumexp(scores, axis=-1, keepdims=True)
    probs = jnp.exp(scores - log_total)
    probs_low = probs.astype(BF16)
    mixed = jnp.einsum("sglm,smd->slgd", probs_low, value, preferred_element_type=F32)
    mixed = mixed.astype(BF16).reshape(rows, q_cols)
    h_own = x_own + rows_back(dot(mixed, out_w, (1, 1), BF16))

    scale_ffn = lax.rsqrt(jnp.mean(h_own * h_own, axis=-1, keepdims=True) + EPS)
    unit_ffn = h_own * scale_ffn
    n2 = whole_rows((unit_ffn * gain_f).astype(BF16))
    logits = dot(n2, router, (1, 1))
    named_all = flags_all[:, :experts] > 0
    kept = flags_all[:, experts : 2 * experts] > 0
    top = jnp.max(jnp.where(named_all, logits, -1e30), axis=1, keepdims=True)
    powers = jnp.where(named_all, jnp.exp(jnp.where(named_all, logits - top, 0.0)), 0.0)
    gates = powers / jnp.maximum(jnp.sum(powers, axis=1, keepdims=True), 1e-30)
    kept_gates = jnp.where(kept, gates, 0.0)

    def spread(per_expert):
        wide = jnp.broadcast_to(per_expert[:, :, None], (rows, experts, hidden_e))
        return jnp.concatenate(
            [wide.reshape(rows, -1), jnp.ones((rows, hidden - experts * hidden_e), F32)], axis=1
        )

    weight = spread(kept_gates)
    ab = dot(n2, up_w, (1, 0))
    a, b = ab[:, :hidden], ab[:, hidden:]
    silu_a = jax.nn.silu(a)
    inner = (silu_a * b).astype(BF16)
    weighted = (weight * inner.astype(F32)).astype(BF16)
    dhid = dot(gy, down_w, (1, 0))
    dgates = jnp.sum(
        (inner.astype(F32) * dhid)[:, : experts * hidden_e].reshape(rows, experts, hidden_e), axis=2
    )
    dgates = jnp.where(kept, dgates, 0.0)
    dlogits = gates * (dgates - jnp.sum(gates * dgates, axis=1, keepdims=True))
    dlogits = dlogits.astype(BF16)
    dinner = weight * dhid
    dab = jnp.concatenate(
        [(dinner * b * silu_slope(a)).astype(BF16), (dinner * silu_a).astype(BF16)], axis=1
    )
    dn2_part = (dot(dab, up_w, (1, 1)) + dot(dlogits, router, (1, 0))).astype(BF16)
    big_ffn = jnp.concatenate(
        [dot(n2, dab, (0, 0), BF16), dot(gy, weighted, (0, 0), BF16)], axis=1
    )
    out_part = dot(weighted, down_w, (1, 1), BF16)
    small_router = dot(dlogits, n2, (0, 0))
    small_ffn = jnp.sum(dn2_part.astype(F32) * n2.astype(F32), axis=0, keepdims=True) / gain_f
    dn2 = rows_back(dn2_part)
    dn2, big_ffn, out_part = lax.optimization_barrier((dn2, big_ffn, out_part))
    near_ffn = xy_scattered(big_ffn)
    scaled = dn2 * gain_f
    dh = gy_own + scale_ffn * (
        scaled - unit_ffn * jnp.mean(scaled * unit_ffn, axis=-1, keepdims=True)
    )

    dattn = whole_rows(dh.astype(BF16))
    dmixed = dot(dattn, out_w, (1, 0), BF16)
    big_out = dot(dattn, mixed, (0, 0), BF16)
    dheads = dmixed.reshape(count, seq_len, GROUP, HEAD_SIZE)
    dprobs = jnp.einsum("slgd,smd->sglm", dheads, value, preferred_element_type=F32)
    dscores = (probs * (dprobs - jnp.sum(probs * dprobs, axis=-1, keepdims=True))).astype(BF16)
    root = 1.0 / math.sqrt(HEAD_SIZE)
    dq = jnp.einsum("sglm,smd->slgd", dscores, key, preferred_element_type=F32) * root
    dk = jnp.einsum("sglm,slgd->smd", dscores, query, preferred_element_type=F32) * root
    dv = jnp.einsum("sglm,slgd->smd", probs_low, dheads, preferred_element_type=F32)
    dqkv = jnp.concatenate(
        [
            dq.astype(BF16).reshape(rows, -1),
            dk.astype(BF16).reshape(rows, -1),
            dv.astype(BF16).reshape(rows, -1),
        ],
        axis=1,
    )
    dn1_part = dot(dqkv, qkv_w, (1, 1), BF16)
    big_attn = jnp.concatenate([dot(n1, dqkv, (0, 0), BF16), big_out], axis=1)
    near_attn = xy_scattered_apart(big_attn)
    small_attn = jnp.sum(dn1_part.astype(F32) * n1.astype(F32), axis=0, keepdims=True) / gain_a
    small = jnp.concatenate([small_attn, small_ffn, small_router], axis=0)
    final = summed_everywhere(to_natural(small))
    dn1 = rows_back(dn1_part)
    scaled = dn1 * gain_a
    dx_own = dh + scale_attn * (
        scaled - unit_attn * jnp.mean(scaled * unit_attn, axis=-1, keepdims=True)
    )
    dx_own = dx_own.astype(BF16)

    def returned(own):
        natural = dot(own, features, (1, 1), BF16).reshape(batches, seq_len, -1)
        sent = jnp.swapaxes(natural, 0, 1).reshape(seq_len, -1, 128)
        got = lax.all_to_all(sent, DP, 0, 0, tiled=True).reshape(seqs, batches, -1)
        back = jnp.einsum("mjs,jmd->msd", deal, got, preferred_element_type=F32)
        return back.astype(BF16)[:, :, None]

    branch = rows_back(out_part)
    out_own = (own_keep * (h_own + branch)).astype(BF16)
    out_tokens = returned(out_own)
    grad_tokens = returned(dx_own)

    def exchanged(near_grads):
        chip = z_scattered(near_grads).reshape(2, rows_here, -1)
        return lax.all_to_all(chip, "c", 0, 0, tiled=True).astype(F32)

    mine = jnp.concatenate([exchanged(near_attn), exchanged(near_ffn)], axis=2)

    def join(start, cols):
        part = mine[:, :, start : start + cols]
        return jnp.swapaxes(part, 0, 1).reshape(rows_here, 2 * cols)

    def join_experts(start):
        part = mine[:, :, start : start + experts * hidden_e]
        part = part.reshape(2, rows_here, experts, hidden_e)
        return jnp.transpose(part, (2, 1, 0, 3)).reshape(experts, rows_here, 2 * hidden_e)

    shared_cols = s_gate.shape[1] // 2
    ffn_at = attn_cols
    each = experts * hidden_e
    return (
        out_tokens,
        grad_tokens,
        final[0],
        final[1],
        join(0, q_cols),
        join(q_cols, k_cols),
        join(q_cols + k_cols, k_cols),
        join(qkv_cols, q_cols).T,
        final[2:].T,
        join_experts(ffn_at),
        join_experts(ffn_at + hidden),
        jnp.swapaxes(join_experts(ffn_at + 2 * hidden), 1, 2),
        join(ffn_at + each, shared_cols),
        join(ffn_at + hidden + each, shared_cols),
        join(ffn_at + 2 * hidden + each, shared_cols).T,
    )


def solution(mesh):
    devices = np.asarray(mesh.devices)
    side = round((devices.shape[0] // 2) ** (1 / 3))
    fine = Mesh(devices.reshape(side, side // 2, 2, side, 2, 2), EVERY)
    rows, cols = P(DP, "zh"), P("zh", DP)
    seqs = P(None, "zh", DP, None)
    return jax.shard_map(
        on_device,
        mesh=fine,
        in_specs=(
            seqs,
            seqs,
            P(),
            P(),
            P(None, None, DP, None),
            P(),
            P(),
            rows,
            rows,
            rows,
            cols,
            P(),
            P(None, DP, "zh"),
            P(None, DP, "zh"),
            P(None, "zh", DP),
            rows,
            rows,
            cols,
        ),
        out_specs=(
            seqs,
            seqs,
            P(),
            P(),
            rows,
            rows,
            rows,
            cols,
            P(),
            P(None, DP, "zh"),
            P(None, DP, "zh"),
            P(None, "zh", DP),
            rows,
            rows,
            cols,
        ),
        check_vma=False,
    )
```

```python
import math

import jax
import jax.numpy as jnp
import numpy as np
from jax import lax
from jax.experimental import pallas as pl
from jax.experimental.pallas import tpu as pltpu
from jax.sharding import Mesh
from jax.sharding import PartitionSpec as P

QUERY_HEAD_COUNT = 12
KEY_VALUE_HEADS = 4
HEAD_SIZE = 128
GROUP = QUERY_HEAD_COUNT // KEY_VALUE_HEADS
CAP = 128
EPS = 1e-06
DP = ("x", "z1", "z0", "y", "c")
EVERY = ("x", "z1", "z0", "y", "c", "zh")
F32 = jnp.float32
BF16 = jnp.bfloat16


def dot(left, right, contract, out=F32):
    result = lax.dot_general(
        left, right, (((contract[0],), (contract[1],)), ((), ())), preferred_element_type=F32
    )
    return result.astype(out)


def swapped(value, axis, bit=1):
    return lax.ppermute(value, axis, [(i, i ^ bit) for i in range(lax.axis_size(axis))])


def whole_rows(own):
    pair = jnp.concatenate([own, swapped(own, "z0")], axis=0)
    return jnp.concatenate([pair, swapped(pair, "c")], axis=0)


def core_sum(part, tied):
    half = part.shape[0] // 2
    both = part[:half].astype(F32) + swapped(part[half:], "c").astype(F32)
    return lax.optimization_barrier((both, tied))


def pair_sum(both):
    quarter = both.shape[0] // 2
    sent = swapped(both[quarter:].astype(BF16), "z0")
    return both[:quarter] + sent.astype(F32)


def z_halves(both):
    halves = both.reshape(2, -1, both.shape[1])
    return jnp.where(lax.axis_index("z0") == 1, halves[::-1], halves)


def rows_back(part, tied=()):
    return pair_sum(core_sum(part, tied)[0])


def z_routes():
    wide = lax.axis_size("z1")
    found = []
    for k1 in range(wide):
        for k2 in range(2):
            pairs = []
            for z1 in range(wide):
                for z0 in range(2):
                    for zh in range(2):
                        goal = ((z1 ^ k1) * 2 + zh) * 2 + (z0 ^ k2)
                        pairs.append(((z1 * 2 + z0) * 2 + zh, goal))
            found.append(pairs)
    return found


def z_gathered(shard):
    return jnp.concatenate(
        [lax.ppermute(shard, ("z1", "z0", "zh"), pairs) for pairs in z_routes()], axis=0
    )


def z_scattered(near, small):
    routes = z_routes()
    rows = near.shape[0] // len(routes)
    cols = near.shape[1]
    pieces = near.reshape(len(routes), rows, cols)
    lines = small.astype(BF16).reshape(rows, -1)
    total = 0.0
    for piece, pairs in zip(pieces, routes):
        back = [(goal, start) for start, goal in pairs]
        sent = jnp.concatenate([piece, lines], axis=1)
        total = total + lax.ppermute(sent, ("z1", "z0", "zh"), back).astype(F32)
    small_sum = total[:, cols:]
    small_sum = small_sum + swapped(small_sum, "c")
    small_sum = small_sum + swapped(small_sum, "zh")
    return total[:, :cols].astype(BF16), small_sum.reshape(small.shape)


def xy_gathered(near):
    return lax.all_gather(near, ("x", "y"), axis=0, tiled=True)


def xy_scattered(total):
    return lax.psum_scatter(total, ("x", "y"), scatter_dimension=0, tiled=True)


def xy_scattered_apart(total, small):
    count = lax.axis_size(("x", "y"))
    cols = total.shape[1]
    pieces = total.reshape(count, -1, cols)
    lines = -(-small.size // (8 * cols)) * 8
    flat = jnp.pad(small.astype(BF16).reshape(-1), (0, lines * cols - small.size))
    flat = jnp.broadcast_to(flat.reshape(1, lines, cols), (count, lines, cols))
    got = lax.all_to_all(jnp.concatenate([pieces, flat], axis=1), ("x", "y"), 0, 0, tiled=True)
    summed = jnp.sum(got.astype(F32), axis=0)
    rows = pieces.shape[1]
    return summed[:rows].astype(BF16), summed[rows:].reshape(-1)[: small.size].reshape(small.shape)


def expert_kernel(
    experts,
    n2_pair_ref,
    n2_other_ref,
    gy_pair_ref,
    gy_other_ref,
    w_ref,
    router_ref,
    n2_ref,
    gy_ref,
    dab_ref,
    weighted_ref,
    dn2_ref,
    out_ref,
    dlogits_ref,
    small_ref,
):
    hidden = weighted_ref.shape[1]
    each = hidden // (experts + 2)
    width = n2_ref.shape[1]
    second = pl.program_id(0) == 1
    n2 = jnp.where(second, n2_other_ref[...], n2_pair_ref[...])
    gy = jnp.where(second, gy_other_ref[:, :width], gy_pair_ref[:, :width])
    flags = jnp.where(second, gy_other_ref[:, width:], gy_pair_ref[:, width:]).astype(F32)
    n2_ref[...] = n2
    gy_ref[...] = gy
    named, kept = flags > 0.5, flags > 1.5
    logits = dot(n2, router_ref[...], (1, 1))
    top = jnp.max(jnp.where(named, logits, -1e30), axis=1, keepdims=True)
    powers = jnp.where(named, jnp.exp(jnp.where(named, logits - top, 0.0)), 0.0)
    gates = powers / jnp.maximum(jnp.sum(powers, axis=1, keepdims=True), 1e-30)
    kept_gates = jnp.where(kept, gates, 0.0)
    lane = lax.broadcasted_iota(jnp.int32, flags.shape, 1)
    dgates = jnp.zeros(flags.shape, F32)
    step = 2 * each
    for at in range(0, hidden, step):
        a = dot(n2, w_ref[:, at : at + step], (1, 0))
        b = dot(n2, w_ref[:, hidden + at : hidden + at + step], (1, 0))
        dhid = dot(gy, w_ref[:, 2 * hidden + at : 2 * hidden + at + step], (1, 0))
        sigma = 1.0 / (1.0 + jnp.exp(-a))
        silu = a * sigma
        inner = (silu * b).astype(BF16).astype(F32)
        first = at // each
        if first < experts:
            scale = jnp.concatenate(
                [
                    jnp.broadcast_to(kept_gates[:, e : e + 1], (flags.shape[0], each))
                    for e in (first, first + 1)
                ],
                axis=1,
            )
            product = inner * dhid
            for e in (first, first + 1):
                lo = (e - first) * each
                total = jnp.sum(product[:, lo : lo + each], axis=1, keepdims=True)
                dgates = jnp.where(lane == e, total, dgates)
            weighted = scale * inner
            dinner = scale * dhid
        else:
            weighted, dinner = inner, dhid
        weighted_ref[:, at : at + step] = weighted.astype(BF16)
        slope = sigma * (1.0 + a * (1.0 - sigma))
        dab_ref[:, at : at + step] = (dinner * b * slope).astype(BF16)
        dab_ref[:, hidden + at : hidden + at + step] = (dinner * silu).astype(BF16)
    dgates = jnp.where(kept, dgates, 0.0)
    dlogits = gates * (dgates - jnp.sum(gates * dgates, axis=1, keepdims=True))
    dlogits = dlogits.astype(BF16)
    dlogits_ref[...] = dlogits
    tile = width // 3
    dab = dab_ref[...]
    weighted = weighted_ref[...]

    @pl.when(pl.program_id(0) == 0)
    def _():
        small_ref[...] = jnp.zeros_like(small_ref)

    for at in range(0, width, tile):
        dn2 = dot(dab, w_ref[at : at + tile, : 2 * hidden], (1, 1))
        dn2 = dn2 + dot(dlogits, router_ref[:, at : at + tile], (1, 0))
        dn2_ref[:, at : at + tile] = dn2.astype(BF16)
        small_ref[:, at : at + tile] += jnp.sum(
            dn2 * n2_ref[:, at : at + tile].astype(F32), axis=0, keepdims=True
        )
        out_ref[:, at : at + tile] = dot(
            weighted, w_ref[at : at + tile, 2 * hidden :], (1, 1), BF16
        )


def experts_both_ways(n2_pair, n2_other, gy_pair, gy_other, ffn_w, router, experts):
    tile, width = n2_pair.shape
    rows = 2 * tile
    hidden = ffn_w.shape[1] // 3

    def by_tile(cols):
        return pl.BlockSpec((tile, cols), lambda i: (i, 0))

    operands = (n2_pair, n2_other, gy_pair, gy_other, ffn_w, router)
    shapes = (width, width, 2 * hidden, hidden, width, width, 128)
    return pl.pallas_call(
        lambda *refs: expert_kernel(experts, *refs),
        grid=(2,),
        in_specs=[
            pl.BlockSpec(v.shape, lambda i: (0, 0), pipeline_mode=pl.Buffered(1)) for v in operands
        ],
        out_specs=[by_tile(n) for n in shapes] + [pl.BlockSpec((1, width), lambda i: (0, 0))],
        out_shape=[jax.ShapeDtypeStruct((rows, n), BF16) for n in shapes]
        + [jax.ShapeDtypeStruct((1, width), F32)],
        compiler_params=pltpu.CompilerParams(vmem_limit_bytes=54 << 20),
        cost_estimate=pl.CostEstimate(
            flops=12 * rows * width * hidden,
            transcendentals=2 * rows * hidden,
            bytes_accessed=2 * (ffn_w.size + rows * (8 * width + 3 * hidden)),
        ),
        name="experts",
    )(*operands)


def attention_backward_kernel(
    seq_len,
    pair_ref,
    other_ref,
    qkv_ref,
    n1_ref,
    w_ref,
    dattn_ref,
    dqkv_ref,
    dn1_ref,
    small_ref,
):
    tile, width = dattn_ref.shape
    cols = dqkv_ref.shape[1]
    q_cols = GROUP * HEAD_SIZE
    root = 1.0 / math.sqrt(HEAD_SIZE)
    dattn = jnp.where(pl.program_id(0) == 1, other_ref[...], pair_ref[...])
    dattn_ref[...] = dattn
    dmixed = dot(dattn, w_ref[:, cols:], (1, 0), BF16)
    row = lax.broadcasted_iota(jnp.int32, (seq_len, seq_len), 0)
    seen = lax.broadcasted_iota(jnp.int32, (seq_len, seq_len), 1) <= row
    for start in range(0, tile, seq_len):
        at = slice(start, start + seq_len)
        key = qkv_ref[at, q_cols : q_cols + HEAD_SIZE]
        value = qkv_ref[at, q_cols + HEAD_SIZE :]
        dkey = jnp.zeros((seq_len, HEAD_SIZE), F32)
        dvalue = jnp.zeros((seq_len, HEAD_SIZE), F32)
        for head in range(0, q_cols, HEAD_SIZE):
            query = qkv_ref[at, head : head + HEAD_SIZE]
            grad = dmixed[at, head : head + HEAD_SIZE]
            scores = jnp.where(seen, dot(query, key, (1, 1)) * root, -1e30)
            powers = jnp.exp(scores - jnp.max(scores, axis=1, keepdims=True))
            probs = powers / jnp.sum(powers, axis=1, keepdims=True)
            dprobs = dot(grad, value, (1, 1))
            inside = jnp.sum(probs * dprobs, axis=1, keepdims=True)
            dscores = (probs * (dprobs - inside)).astype(BF16)
            dqkv_ref[at, head : head + HEAD_SIZE] = (dot(dscores, key, (1, 0)) * root).astype(BF16)
            dkey = dkey + dot(dscores, query, (0, 0))
            dvalue = dvalue + dot(probs.astype(BF16), grad, (0, 0))
        dqkv_ref[at, q_cols : q_cols + HEAD_SIZE] = (dkey * root).astype(BF16)
        dqkv_ref[at, q_cols + HEAD_SIZE :] = dvalue.astype(BF16)
    dqkv = dqkv_ref[...]

    @pl.when(pl.program_id(0) == 0)
    def _():
        small_ref[...] = jnp.zeros_like(small_ref)

    step = width // 3
    for at in range(0, width, step):
        dn1 = dot(dqkv, w_ref[at : at + step, :cols], (1, 1))
        dn1_ref[:, at : at + step] = dn1.astype(BF16)
        small_ref[:, at : at + step] += jnp.sum(
            dn1 * n1_ref[:, at : at + step].astype(F32), axis=0, keepdims=True
        )


def attention_backward(pair, other, qkv, n1, attn_w, seq_len):
    tile, width = pair.shape
    rows, cols = qkv.shape

    def whole(value):
        return pl.BlockSpec(value.shape, lambda i: (0, 0), pipeline_mode=pl.Buffered(1))

    def by_tile(cols):
        return pl.BlockSpec((tile, cols), lambda i: (i, 0))

    return pl.pallas_call(
        lambda *refs: attention_backward_kernel(seq_len, *refs),
        grid=(2,),
        in_specs=[whole(pair), whole(other), by_tile(cols), by_tile(width), whole(attn_w)],
        out_specs=[
            by_tile(width),
            by_tile(cols),
            by_tile(width),
            pl.BlockSpec((1, width), lambda i: (0, 0)),
        ],
        out_shape=[jax.ShapeDtypeStruct((rows, n), BF16) for n in (width, cols, width)]
        + [jax.ShapeDtypeStruct((1, width), F32)],
        compiler_params=pltpu.CompilerParams(vmem_limit_bytes=44 << 20),
        cost_estimate=pl.CostEstimate(
            flops=2 * rows * width * attn_w.shape[1],
            transcendentals=rows * seq_len * GROUP,
            bytes_accessed=2 * (attn_w.size + rows * (5 * width + 2 * cols)),
        ),
        name="attention_backward",
    )(pair, other, qkv, n1, attn_w)


def attention_scores(query, key):
    scaled = jnp.einsum("slgd,smd->sglm", query, key, preferred_element_type=F32) * (
        1.0 / math.sqrt(HEAD_SIZE)
    )
    place = jnp.arange(query.shape[1], dtype=jnp.int32)
    return jnp.where(place[None, :] <= place[:, None], scaled, -1e30)


def on_device(
    tokens,
    cotangent,
    lengths,
    perm,
    routes,
    gain_attn,
    gain_ffn,
    query_matrix,
    key_matrix,
    value_matrix,
    w_out,
    w_router,
    w_gate,
    w_up,
    w_down,
    s_gate,
    s_up,
    s_down,
):
    t = lax.axis_index("zh")
    place_here = lax.axis_index(DP)
    side_x, side_z1, side_z0, side_y = (lax.axis_size(a) for a in ("x", "z1", "z0", "y"))
    side_zl = side_z1 * side_z0
    flips = (lax.axis_index("z1"), t)
    batches, seqs = tokens.shape[0], tokens.shape[1]
    seq_len = lax.axis_size(DP)
    width = tokens.shape[3]
    experts = w_gate.shape[0]
    rows_here = query_matrix.shape[0]

    def halves(value):
        cols = value.shape[-1] // 2
        return value[..., :cols], value[..., cols:]

    def by_row(value):
        return jnp.concatenate([value[e] for e in range(experts)], axis=1)

    attn_parts = [halves(v) for v in (query_matrix, key_matrix, value_matrix, w_out.T)]
    ffn_parts = [
        tuple(by_row(v) for v in halves(w_gate)),
        halves(s_gate),
        tuple(by_row(v) for v in halves(w_up)),
        halves(s_up),
        tuple(by_row(v) for v in halves(jnp.swapaxes(w_down, 1, 2))),
        halves(s_down.T),
    ]
    attn_cols = sum(p[0].shape[1] for p in attn_parts)
    both_shards = jnp.stack(
        [jnp.concatenate([p[c] for p in attn_parts + ffn_parts], axis=1) for c in (0, 1)]
    )
    chip_rows = lax.all_to_all(both_shards, "c", 0, 0, tiled=True)
    chip_rows = chip_rows.reshape(2 * rows_here, -1)
    near_w = z_gathered(chip_rows)
    q_cols = query_matrix.shape[1] // 2
    k_cols = key_matrix.shape[1] // 2
    qkv_cols = q_cols + 2 * k_cols
    hidden_e = w_gate.shape[2] // 2
    hidden = experts * hidden_e + s_gate.shape[1] // 2

    def flipped(value, axes):
        for axis, flip in zip(axes, flips):
            value = jnp.where(flip == 1, jnp.flip(value, axis), value)
        return value

    def to_local(value):
        parts = value.reshape(-1, side_x, side_z1, side_z0, side_y, width // (seq_len // 2))
        return flipped(jnp.transpose(parts, (0, 1, 4, 2, 3, 5)), (3, 4)).reshape(value.shape)

    def to_natural(value):
        parts = value.reshape(-1, side_x, side_y, side_z1, side_z0, width // (seq_len // 2))
        return jnp.transpose(flipped(parts, (3, 4)), (0, 1, 3, 4, 2, 5)).reshape(value.shape)

    unit = width // (seq_len // 2)
    iota = jnp.arange(width, dtype=jnp.int32)
    piece = iota // unit
    zl_of = (piece % side_zl) ^ (flips[0] * 2 + flips[1])
    mate = (
        ((piece // (side_zl * side_y)) * side_zl + zl_of) * side_y + (piece // side_zl) % side_y
    ) * unit + iota % unit
    features = (iota[:, None] == mate[None, :]).astype(BF16)

    order = lax.dynamic_index_in_dim(perm, t, 1, False)
    deal = (order[:, :, None] == jnp.arange(seqs, dtype=jnp.int32)[None, None, :]).astype(BF16)
    own_routes = lax.dynamic_slice_in_dim(routes[:, :, 0], t * seqs, seqs, 1)
    own_lengths = lax.dynamic_slice_in_dim(lengths, t * seqs, seqs, 1)
    own_valid = place_here < own_lengths
    named = jnp.any(
        own_routes[:, :, :, None] == jnp.arange(experts, dtype=jnp.int32), axis=2
    )
    marks = jnp.concatenate(
        [jnp.logical_and(named, own_valid[:, :, None]), own_valid[:, :, None]], axis=2
    ).astype(BF16)
    marks = jnp.pad(marks, ((0, 0), (0, 0), (0, 128 - marks.shape[2])))
    rows_in = jnp.concatenate([tokens[:, :, 0], marks, cotangent[:, :, 0]], axis=2)
    sent = jnp.einsum("mjs,msd->jmd", deal, rows_in, preferred_element_type=F32)
    sent = sent.astype(BF16).reshape(seqs, -1, 128)
    near_w, sent = lax.optimization_barrier((near_w, sent))
    attn_w = xy_gathered(near_w[:, :attn_cols])
    ffn_w = xy_gathered(near_w[:, attn_cols:])
    qkv_w, out_w = attn_w[:, :qkv_cols], attn_w[:, qkv_cols:]
    got = lax.all_to_all(sent, DP, 0, 0, tiled=True)
    got = got.reshape(seq_len, batches, -1)
    own_in = jnp.swapaxes(got, 0, 1)
    x_own = dot(own_in[:, :, :width].reshape(batches * seq_len, width), features, (1, 0))
    own_marks = own_in[:, :, width : width + 128]
    own_hits = own_marks[:, :, :experts]
    own_keep = own_marks[:, :, experts].reshape(-1, 1).astype(F32)
    gy_own = own_keep * dot(
        own_in[:, :, width + 128 :].reshape(batches * seq_len, width), features, (1, 0)
    )

    place = jnp.arange(seq_len, dtype=jnp.int32)
    earlier = (place[None, :] < place[:, None]).astype(BF16)
    before = jnp.einsum("pq,mqe->mpe", earlier, own_hits, preferred_element_type=F32)
    totals = jnp.sum(own_hits.astype(F32), axis=1)
    other_totals = swapped(totals, "zh")
    rank = before + jnp.where(t == 1, other_totals, 0.0)[:, None, :]
    own_kept = jnp.where(rank < CAP, own_hits, jnp.zeros_like(own_hits))
    flags = (own_hits + own_kept).reshape(batches * seq_len, -1)
    flags = jnp.pad(flags, ((0, 0), (0, 128 - flags.shape[1])))

    def to_send(own):
        natural = dot(own, features, (1, 1), BF16).reshape(batches, seq_len, -1)
        return jnp.swapaxes(natural, 0, 1).reshape(seq_len, -1, 128)

    def placed(got):
        got = got.reshape(seqs, batches, -1)
        back = jnp.einsum("mjs,jmd->msd", deal, got, preferred_element_type=F32)
        return back.astype(BF16)[:, :, None]

    small_in = to_local(
        jnp.concatenate([gain_attn[None], gain_ffn[None], w_router.T.astype(F32)], axis=0)
    )
    gain_a, gain_f, router = small_in[0:1], small_in[1:2], small_in[2:].astype(BF16)
    scale_attn = lax.rsqrt(jnp.mean(x_own * x_own, axis=-1, keepdims=True) + EPS)
    unit_attn = x_own * scale_attn
    n1_own = (unit_attn * gain_a).astype(BF16)
    gy_own_low = jnp.concatenate([gy_own.astype(BF16), flags], axis=1)
    n1_other, gy_own_low = lax.optimization_barrier((swapped(n1_own, "z0"), gy_own_low))
    n1 = jnp.concatenate([n1_own, n1_other], axis=0)
    n1 = jnp.concatenate([n1, swapped(n1, "c")], axis=0)
    gy_pair = lax.all_to_all(
        jnp.broadcast_to(gy_own_low[None], (2, *gy_own_low.shape)), "z0", 0, 0, tiled=True
    )
    rows = n1.shape[0]
    count = rows // seq_len
    qkv = dot(n1, qkv_w, (1, 0), BF16)
    query = qkv[:, :q_cols].reshape(count, seq_len, GROUP, HEAD_SIZE)
    key = qkv[:, q_cols : q_cols + k_cols].reshape(count, seq_len, HEAD_SIZE)
    value = qkv[:, q_cols + k_cols :].reshape(count, seq_len, HEAD_SIZE)
    scores = attention_scores(query, key)
    log_total = jax.nn.logsumexp(scores, axis=-1, keepdims=True)
    probs = jnp.exp(scores - log_total)
    probs_low = probs.astype(BF16)
    mixed = jnp.einsum("sglm,smd->slgd", probs_low, value, preferred_element_type=F32)
    mixed = mixed.astype(BF16).reshape(rows, q_cols)
    mixed, gy_pair = lax.optimization_barrier((mixed, gy_pair))
    gy_pair = jnp.where(lax.axis_index("z0") == 1, gy_pair[::-1], gy_pair)
    gy_pair = gy_pair.reshape(-1, gy_own_low.shape[1])
    gy_other = swapped(gy_pair, "c")
    h_own = x_own + rows_back(dot(mixed, out_w, (1, 1), BF16))

    scale_ffn = lax.rsqrt(jnp.mean(h_own * h_own, axis=-1, keepdims=True) + EPS)
    unit_ffn = h_own * scale_ffn
    n2_own = (unit_ffn * gain_f).astype(BF16)
    n2_pair = jnp.concatenate([n2_own, swapped(n2_own, "z0")], axis=0)
    n2_other = swapped(n2_pair, "c")
    router_low = jnp.pad(router, ((0, 128 - experts), (0, 0)))
    n2, gy, dab, weighted, dn2_part, out_part, dlogits, small_ffn = experts_both_ways(
        n2_pair, n2_other, gy_pair, gy_other, ffn_w, router_low, experts
    )
    big_down = dot(gy, weighted, (0, 0), BF16)
    dn2_sum, dab = core_sum(dn2_part, dab)
    dn2 = pair_sum(dn2_sum)
    big_ffn = jnp.concatenate([dot(n2, dab, (0, 0), BF16), big_down], axis=1)
    small_router = dot(dlogits, n2, (0, 0))[:experts]
    small_ffn = small_ffn / gain_f
    dn2, big_ffn = lax.optimization_barrier((dn2, big_ffn))
    near_ffn = xy_scattered(big_ffn)
    scaled = dn2 * gain_f
    dh = gy_own + scale_ffn * (
        scaled - unit_ffn * jnp.mean(scaled * unit_ffn, axis=-1, keepdims=True)
    )

    dattn_own, out_part = lax.optimization_barrier((dh.astype(BF16), out_part))
    out_halves = z_halves(core_sum(out_part, ())[0].astype(BF16))
    dattn_other, small_router, out_halves = lax.optimization_barrier(
        (swapped(dattn_own, "z0"), small_router, out_halves)
    )
    dattn_pair = jnp.concatenate([dattn_own, dattn_other], axis=0)
    dattn, dqkv, dn1_part, small_attn = attention_backward(
        dattn_pair, swapped(dattn_pair, "c"), qkv, n1, attn_w, seq_len
    )
    dqkv, halves_got = lax.optimization_barrier(
        (dqkv, lax.all_to_all(out_halves, "z0", 0, 0, tiled=True))
    )
    branch = jnp.sum(halves_got.astype(F32), axis=0)
    out_own = (own_keep * (h_own + branch)).astype(BF16)
    out_got = lax.all_to_all(to_send(out_own), DP, 0, 0, tiled=True)
    big_attn = jnp.concatenate([dot(n1, dqkv, (0, 0), BF16), dot(dattn, mixed, (0, 0), BF16)], axis=1)
    small = jnp.concatenate([small_attn / gain_a, small_ffn, small_router], axis=0)
    dn1_sum, big_attn = core_sum(dn1_part, big_attn)
    dn1 = pair_sum(dn1_sum)
    scaled = dn1 * gain_a
    dx_own = dh + scale_attn * (
        scaled - unit_attn * jnp.mean(scaled * unit_attn, axis=-1, keepdims=True)
    )
    big_attn, out_got = lax.optimization_barrier((big_attn, out_got))
    near_attn, small = xy_scattered_apart(big_attn, to_natural(small))
    dx_own, near_ffn = lax.optimization_barrier((dx_own.astype(BF16), near_ffn))
    dx_got = lax.all_to_all(to_send(dx_own), DP, 0, 0, tiled=True)

    chip, final = z_scattered(jnp.concatenate([near_attn, near_ffn], axis=1), small)
    chip, dx_got = lax.optimization_barrier((chip, dx_got))
    out_tokens, grad_tokens = placed(out_got), placed(dx_got)
    mine = lax.all_to_all(chip.reshape(2, rows_here, -1), "c", 0, 0, tiled=True).astype(F32)

    def join(start, cols):
        part = mine[:, :, start : start + cols]
        return jnp.swapaxes(part, 0, 1).reshape(rows_here, 2 * cols)

    def join_experts(start):
        part = mine[:, :, start : start + experts * hidden_e]
        part = part.reshape(2, rows_here, experts, hidden_e)
        return jnp.transpose(part, (2, 1, 0, 3)).reshape(experts, rows_here, 2 * hidden_e)

    shared_cols = s_gate.shape[1] // 2
    ffn_at = attn_cols
    each = experts * hidden_e
    return (
        out_tokens,
        grad_tokens,
        final[0],
        final[1],
        join(0, q_cols),
        join(q_cols, k_cols),
        join(q_cols + k_cols, k_cols),
        join(qkv_cols, q_cols).T,
        final[2:].T,
        join_experts(ffn_at),
        join_experts(ffn_at + hidden),
        jnp.swapaxes(join_experts(ffn_at + 2 * hidden), 1, 2),
        join(ffn_at + each, shared_cols),
        join(ffn_at + hidden + each, shared_cols),
        join(ffn_at + 2 * hidden + each, shared_cols).T,
    )


def solution(mesh):
    devices = np.asarray(mesh.devices)
    side = round((devices.shape[0] // 2) ** (1 / 3))
    fine = Mesh(devices.reshape(side, side // 2, 2, side, 2, 2), EVERY)
    rows, cols = P(DP, "zh"), P("zh", DP)
    seqs = P(None, "zh", DP, None)
    return jax.shard_map(
        on_device,
        mesh=fine,
        in_specs=(
            seqs,
            seqs,
            P(),
            P(),
            P(None, None, DP, None),
            P(),
            P(),
            rows,
            rows,
            rows,
            cols,
            P(),
            P(None, DP, "zh"),
            P(None, DP, "zh"),
            P(None, "zh", DP),
            rows,
            rows,
            cols,
        ),
        out_specs=(
            seqs,
            seqs,
            P(),
            P(),
            rows,
            rows,
            rows,
            cols,
            P(),
            P(None, DP, "zh"),
            P(None, DP, "zh"),
            P(None, "zh", DP),
            rows,
            rows,
            cols,
        ),
        check_vma=False,
    )
```

```python
import math

import jax
import jax.numpy as jnp
import numpy as np
from jax import lax
from jax.experimental import pallas as pl
from jax.experimental.pallas import tpu as pltpu
from jax.sharding import Mesh
from jax.sharding import PartitionSpec as P

QUERY_HEAD_COUNT = 12
KEY_VALUE_HEADS = 4
HEAD_SIZE = 128
GROUP = QUERY_HEAD_COUNT // KEY_VALUE_HEADS
CAP = 128
EPS = 1e-06
DP = ("x", "z1", "z0", "y", "c")
EVERY = ("x", "z1", "z0", "y", "c", "zh")
F32 = jnp.float32
BF16 = jnp.bfloat16


def dot(left, right, contract, out=F32):
    result = lax.dot_general(
        left, right, (((contract[0],), (contract[1],)), ((), ())), preferred_element_type=F32
    )
    return result.astype(out)


def swapped(value, axis, bit=1):
    return lax.ppermute(value, axis, [(i, i ^ bit) for i in range(lax.axis_size(axis))])


def whole_rows(own):
    pair = jnp.concatenate([own, swapped(own, "z0")], axis=0)
    return jnp.concatenate([pair, swapped(pair, "c")], axis=0)


def core_sum(part, tied):
    half = part.shape[0] // 2
    both = part[:half].astype(F32) + swapped(part[half:], "c").astype(F32)
    return lax.optimization_barrier((both, tied))


def pair_sum(both):
    quarter = both.shape[0] // 2
    sent = swapped(both[quarter:].astype(BF16), "z0")
    return both[:quarter] + sent.astype(F32)


def z_halves(both):
    halves = both.reshape(2, -1, both.shape[1])
    return jnp.where(lax.axis_index("z0") == 1, halves[::-1], halves)


def rows_back(part, tied=()):
    return pair_sum(core_sum(part, tied)[0])


def z_routes():
    wide = lax.axis_size("z1")
    found = []
    for k1 in range(wide):
        for k2 in range(2):
            pairs = []
            for z1 in range(wide):
                for z0 in range(2):
                    for zh in range(2):
                        goal = ((z1 ^ k1) * 2 + zh) * 2 + (z0 ^ k2)
                        pairs.append(((z1 * 2 + z0) * 2 + zh, goal))
            found.append(pairs)
    return found


def z_gathered(shard):
    return jnp.concatenate(
        [lax.ppermute(shard, ("z1", "z0", "zh"), pairs) for pairs in z_routes()], axis=0
    )


def z_scattered(near):
    routes = z_routes()
    pieces = near.reshape(len(routes), -1, near.shape[1])
    total = 0.0
    for piece, pairs in zip(pieces, routes):
        back = [(goal, start) for start, goal in pairs]
        total = total + lax.ppermute(piece, ("z1", "z0", "zh"), back).astype(F32)
    return total


def xy_gathered(near):
    return lax.all_gather(near, ("x", "y"), axis=0, tiled=True)


def xy_scattered(total):
    return lax.psum_scatter(total, ("x", "y"), scatter_dimension=0, tiled=True)


def in_lines(small, cols):
    first = min(small.shape[1], cols)
    lines = jnp.pad(small[:, :first], ((0, 0), (0, cols - first)))
    lines = jnp.concatenate([lines, small[:, first:].reshape(-1, cols)], axis=0)
    return jnp.pad(lines, ((0, 16 - lines.shape[0]), (0, 0)))


def from_lines(lines, rows, width):
    first = min(width, lines.shape[1])
    rest = lines[rows : rows + rows * (width - first) // lines.shape[1]]
    return jnp.concatenate([lines[:rows, :first], rest.reshape(rows, -1)], axis=1)


def expert_kernel(
    experts,
    n2_pair_ref,
    n2_other_ref,
    gy_pair_ref,
    gy_other_ref,
    w_ref,
    router_ref,
    n2_ref,
    gy_ref,
    dab_ref,
    weighted_ref,
    dn2_ref,
    out_ref,
    dlogits_ref,
    small_ref,
):
    hidden = weighted_ref.shape[1]
    each = hidden // (experts + 2)
    width = n2_ref.shape[1]
    second = pl.program_id(0) == 1
    n2 = jnp.where(second, n2_other_ref[...], n2_pair_ref[...])
    gy = jnp.where(second, gy_other_ref[:, :width], gy_pair_ref[:, :width])
    flags = jnp.where(second, gy_other_ref[:, width:], gy_pair_ref[:, width:]).astype(F32)
    n2_ref[...] = n2
    gy_ref[...] = gy
    named, kept = flags > 0.5, flags > 1.5
    logits = dot(n2, router_ref[...], (1, 1))
    top = jnp.max(jnp.where(named, logits, -1e30), axis=1, keepdims=True)
    powers = jnp.where(named, jnp.exp(jnp.where(named, logits - top, 0.0)), 0.0)
    gates = powers / jnp.maximum(jnp.sum(powers, axis=1, keepdims=True), 1e-30)
    kept_gates = jnp.where(kept, gates, 0.0)
    lane = lax.broadcasted_iota(jnp.int32, flags.shape, 1)
    dgates = jnp.zeros(flags.shape, F32)
    step = 2 * each
    for at in range(0, hidden, step):
        a = dot(n2, w_ref[:, at : at + step], (1, 0))
        b = dot(n2, w_ref[:, hidden + at : hidden + at + step], (1, 0))
        dhid = dot(gy, w_ref[:, 2 * hidden + at : 2 * hidden + at + step], (1, 0))
        sigma = 1.0 / (1.0 + jnp.exp(-a))
        silu = a * sigma
        inner = (silu * b).astype(BF16).astype(F32)
        first = at // each
        if first < experts:
            scale = jnp.concatenate(
                [
                    jnp.broadcast_to(kept_gates[:, e : e + 1], (flags.shape[0], each))
                    for e in (first, first + 1)
                ],
                axis=1,
            )
            product = inner * dhid
            for e in (first, first + 1):
                lo = (e - first) * each
                total = jnp.sum(product[:, lo : lo + each], axis=1, keepdims=True)
                dgates = jnp.where(lane == e, total, dgates)
            weighted = scale * inner
            dinner = scale * dhid
        else:
            weighted, dinner = inner, dhid
        weighted_ref[:, at : at + step] = weighted.astype(BF16)
        slope = sigma * (1.0 + a * (1.0 - sigma))
        dab_ref[:, at : at + step] = (dinner * b * slope).astype(BF16)
        dab_ref[:, hidden + at : hidden + at + step] = (dinner * silu).astype(BF16)
    dgates = jnp.where(kept, dgates, 0.0)
    dlogits = gates * (dgates - jnp.sum(gates * dgates, axis=1, keepdims=True))
    dlogits = dlogits.astype(BF16)
    dlogits_ref[...] = dlogits
    tile = width // 3
    dab = dab_ref[...]
    weighted = weighted_ref[...]

    @pl.when(pl.program_id(0) == 0)
    def _():
        small_ref[...] = jnp.zeros_like(small_ref)

    for at in range(0, width, tile):
        dn2 = dot(dab, w_ref[at : at + tile, : 2 * hidden], (1, 1))
        dn2 = dn2 + dot(dlogits, router_ref[:, at : at + tile], (1, 0))
        dn2_ref[:, at : at + tile] = dn2.astype(BF16)
        small_ref[:, at : at + tile] += jnp.sum(
            dn2 * n2_ref[:, at : at + tile].astype(F32), axis=0, keepdims=True
        )
        out_ref[:, at : at + tile] = dot(
            weighted, w_ref[at : at + tile, 2 * hidden :], (1, 1), BF16
        )


def experts_both_ways(n2_pair, n2_other, gy_pair, gy_other, ffn_w, router, experts):
    tile, width = n2_pair.shape
    rows = 2 * tile
    hidden = ffn_w.shape[1] // 3

    def by_tile(cols):
        return pl.BlockSpec((tile, cols), lambda i: (i, 0))

    operands = (n2_pair, n2_other, gy_pair, gy_other, ffn_w, router)
    shapes = (width, width, 2 * hidden, hidden, width, width, 128)
    return pl.pallas_call(
        lambda *refs: expert_kernel(experts, *refs),
        grid=(2,),
        in_specs=[
            pl.BlockSpec(v.shape, lambda i: (0, 0), pipeline_mode=pl.Buffered(1)) for v in operands
        ],
        out_specs=[by_tile(n) for n in shapes] + [pl.BlockSpec((1, width), lambda i: (0, 0))],
        out_shape=[jax.ShapeDtypeStruct((rows, n), BF16) for n in shapes]
        + [jax.ShapeDtypeStruct((1, width), F32)],
        compiler_params=pltpu.CompilerParams(vmem_limit_bytes=54 << 20),
        cost_estimate=pl.CostEstimate(
            flops=12 * rows * width * hidden,
            transcendentals=2 * rows * hidden,
            bytes_accessed=2 * (ffn_w.size + rows * (8 * width + 3 * hidden)),
        ),
        name="experts",
    )(*operands)


def attention_backward_kernel(
    seq_len,
    pair_ref,
    other_ref,
    qkv_ref,
    n1_ref,
    w_ref,
    dattn_ref,
    dqkv_ref,
    dn1_ref,
    small_ref,
):
    tile, width = dattn_ref.shape
    cols = dqkv_ref.shape[1]
    q_cols = GROUP * HEAD_SIZE
    root = 1.0 / math.sqrt(HEAD_SIZE)
    dattn = jnp.where(pl.program_id(0) == 1, other_ref[...], pair_ref[...])
    dattn_ref[...] = dattn
    dmixed = dot(dattn, w_ref[:, cols:], (1, 0), BF16)
    row = lax.broadcasted_iota(jnp.int32, (seq_len, seq_len), 0)
    seen = lax.broadcasted_iota(jnp.int32, (seq_len, seq_len), 1) <= row
    for start in range(0, tile, seq_len):
        at = slice(start, start + seq_len)
        key = qkv_ref[at, q_cols : q_cols + HEAD_SIZE]
        value = qkv_ref[at, q_cols + HEAD_SIZE :]
        dkey = jnp.zeros((seq_len, HEAD_SIZE), F32)
        dvalue = jnp.zeros((seq_len, HEAD_SIZE), F32)
        for head in range(0, q_cols, HEAD_SIZE):
            query = qkv_ref[at, head : head + HEAD_SIZE]
            grad = dmixed[at, head : head + HEAD_SIZE]
            scores = jnp.where(seen, dot(query, key, (1, 1)) * root, -1e30)
            powers = jnp.exp(scores - jnp.max(scores, axis=1, keepdims=True))
            probs = powers / jnp.sum(powers, axis=1, keepdims=True)
            dprobs = dot(grad, value, (1, 1))
            inside = jnp.sum(probs * dprobs, axis=1, keepdims=True)
            dscores = (probs * (dprobs - inside)).astype(BF16)
            dqkv_ref[at, head : head + HEAD_SIZE] = (dot(dscores, key, (1, 0)) * root).astype(BF16)
            dkey = dkey + dot(dscores, query, (0, 0))
            dvalue = dvalue + dot(probs.astype(BF16), grad, (0, 0))
        dqkv_ref[at, q_cols : q_cols + HEAD_SIZE] = (dkey * root).astype(BF16)
        dqkv_ref[at, q_cols + HEAD_SIZE :] = dvalue.astype(BF16)
    dqkv = dqkv_ref[...]

    @pl.when(pl.program_id(0) == 0)
    def _():
        small_ref[...] = jnp.zeros_like(small_ref)

    step = width // 3
    for at in range(0, width, step):
        dn1 = dot(dqkv, w_ref[at : at + step, :cols], (1, 1))
        dn1_ref[:, at : at + step] = dn1.astype(BF16)
        small_ref[:, at : at + step] += jnp.sum(
            dn1 * n1_ref[:, at : at + step].astype(F32), axis=0, keepdims=True
        )


def attention_backward(pair, other, qkv, n1, attn_w, seq_len):
    tile, width = pair.shape
    rows, cols = qkv.shape

    def whole(value):
        return pl.BlockSpec(value.shape, lambda i: (0, 0), pipeline_mode=pl.Buffered(1))

    def by_tile(cols):
        return pl.BlockSpec((tile, cols), lambda i: (i, 0))

    return pl.pallas_call(
        lambda *refs: attention_backward_kernel(seq_len, *refs),
        grid=(2,),
        in_specs=[whole(pair), whole(other), by_tile(cols), by_tile(width), whole(attn_w)],
        out_specs=[
            by_tile(width),
            by_tile(cols),
            by_tile(width),
            pl.BlockSpec((1, width), lambda i: (0, 0)),
        ],
        out_shape=[jax.ShapeDtypeStruct((rows, n), BF16) for n in (width, cols, width)]
        + [jax.ShapeDtypeStruct((1, width), F32)],
        compiler_params=pltpu.CompilerParams(vmem_limit_bytes=44 << 20),
        cost_estimate=pl.CostEstimate(
            flops=12 * rows * width * attn_w.shape[1],
            transcendentals=rows * seq_len * GROUP,
            bytes_accessed=2 * (attn_w.size + rows * (5 * width + 2 * cols)),
        ),
        name="attention_backward",
    )(pair, other, qkv, n1, attn_w)


def gradients_kernel(n1_ref, dattn_ref, dqkv_ref, mixed_ref, lines_ref, out_ref):
    blocks = out_ref.shape[0]
    rows = n1_ref.shape[1] // blocks
    split = dqkv_ref.shape[1]
    qkv = dot(n1_ref[...], dqkv_ref[...], (0, 0), BF16)
    out = dot(dattn_ref[...], mixed_ref[...], (0, 0), BF16)
    for b in range(blocks):
        out_ref[b, :rows, :split] = qkv[b * rows : (b + 1) * rows]
        out_ref[b, :rows, split:] = out[b * rows : (b + 1) * rows]
        out_ref[b, rows:, :] = lines_ref[...]


def attention_gradients(n1, dqkv, dattn, mixed, small, places):
    rows, width = n1.shape
    cols = dqkv.shape[1] + mixed.shape[1]
    lines = width // places + small.shape[0]
    step = width // 4

    def whole(value):
        return pl.BlockSpec(value.shape, lambda i: (0, 0), pipeline_mode=pl.Buffered(1))

    by_features = pl.BlockSpec((rows, step), lambda i: (0, i))
    return pl.pallas_call(
        gradients_kernel,
        grid=(4,),
        in_specs=[by_features, by_features, whole(dqkv), whole(mixed), whole(small)],
        out_specs=pl.BlockSpec((places // 4, lines, cols), lambda i: (i, 0, 0)),
        out_shape=jax.ShapeDtypeStruct((places, lines, cols), BF16),
        compiler_params=pltpu.CompilerParams(vmem_limit_bytes=40 << 20),
        cost_estimate=pl.CostEstimate(
            flops=2 * rows * width * cols,
            transcendentals=0,
            bytes_accessed=2 * (2 * rows * width + rows * cols + places * lines * cols),
        ),
        name="attention_gradients",
    )(n1, dattn, dqkv, mixed, small)


def attention_scores(query, key):
    scaled = jnp.einsum("slgd,smd->sglm", query, key, preferred_element_type=F32) * (
        1.0 / math.sqrt(HEAD_SIZE)
    )
    place = jnp.arange(query.shape[1], dtype=jnp.int32)
    return jnp.where(place[None, :] <= place[:, None], scaled, -1e30)


def on_device(
    tokens,
    cotangent,
    lengths,
    perm,
    routes,
    gain_attn,
    gain_ffn,
    query_matrix,
    key_matrix,
    value_matrix,
    w_out,
    w_router,
    w_gate,
    w_up,
    w_down,
    s_gate,
    s_up,
    s_down,
):
    t = lax.axis_index("zh")
    place_here = lax.axis_index(DP)
    side_x, side_z1, side_z0, side_y = (lax.axis_size(a) for a in ("x", "z1", "z0", "y"))
    side_zl = side_z1 * side_z0
    flips = (lax.axis_index("z1"), t)
    batches, seqs = tokens.shape[0], tokens.shape[1]
    seq_len = lax.axis_size(DP)
    width = tokens.shape[3]
    experts = w_gate.shape[0]
    rows_here = query_matrix.shape[0]

    def halves(value):
        cols = value.shape[-1] // 2
        return value[..., :cols], value[..., cols:]

    def by_row(value):
        return jnp.concatenate([value[e] for e in range(experts)], axis=1)

    attn_parts = [halves(v) for v in (query_matrix, key_matrix, value_matrix, w_out.T)]
    ffn_parts = [
        tuple(by_row(v) for v in halves(w_gate)),
        halves(s_gate),
        tuple(by_row(v) for v in halves(w_up)),
        halves(s_up),
        tuple(by_row(v) for v in halves(jnp.swapaxes(w_down, 1, 2))),
        halves(s_down.T),
    ]
    attn_cols = sum(p[0].shape[1] for p in attn_parts)
    q_cols = query_matrix.shape[1] // 2
    k_cols = key_matrix.shape[1] // 2
    qkv_cols = q_cols + 2 * k_cols
    hidden_e = w_gate.shape[2] // 2
    hidden = experts * hidden_e + s_gate.shape[1] // 2

    def flipped(value, axes):
        for axis, flip in zip(axes, flips):
            value = jnp.where(flip == 1, jnp.flip(value, axis), value)
        return value

    def to_local(value):
        parts = value.reshape(-1, side_x, side_z1, side_z0, side_y, width // (seq_len // 2))
        return flipped(jnp.transpose(parts, (0, 1, 4, 2, 3, 5)), (3, 4)).reshape(value.shape)

    def to_natural(value):
        parts = value.reshape(-1, side_x, side_y, side_z1, side_z0, width // (seq_len // 2))
        return jnp.transpose(flipped(parts, (3, 4)), (0, 1, 3, 4, 2, 5)).reshape(value.shape)

    unit = width // (seq_len // 2)
    iota = jnp.arange(width, dtype=jnp.int32)
    piece = iota // unit
    zl_of = (piece % side_zl) ^ (flips[0] * 2 + flips[1])
    mate = (
        ((piece // (side_zl * side_y)) * side_zl + zl_of) * side_y + (piece // side_zl) % side_y
    ) * unit + iota % unit
    features = (iota[:, None] == mate[None, :]).astype(BF16)

    def both_cores(chip):
        low = chip.astype(BF16)
        kept = jnp.where(core == 0, low[:rows_here], low[rows_here:])
        got = swapped(jnp.where(core == 0, low[rows_here:], low[:rows_here]), "c")
        pair = jnp.where(core == 0, jnp.stack([kept, got]), jnp.stack([got, kept]))
        return pair.astype(F32)

    order = lax.dynamic_index_in_dim(perm, t, 1, False)
    deal = (order[:, :, None] == jnp.arange(seqs, dtype=jnp.int32)[None, None, :]).astype(BF16)
    own_routes = lax.dynamic_slice_in_dim(routes[:, :, 0], t * seqs, seqs, 1)
    own_lengths = lax.dynamic_slice_in_dim(lengths, t * seqs, seqs, 1)
    own_valid = place_here < own_lengths
    named = jnp.any(
        own_routes[:, :, :, None] == jnp.arange(experts, dtype=jnp.int32), axis=2
    )
    marks = jnp.concatenate(
        [jnp.logical_and(named, own_valid[:, :, None]), own_valid[:, :, None]], axis=2
    ).astype(BF16)
    marks = jnp.pad(marks, ((0, 0), (0, 0), (0, 128 - marks.shape[2])))

    def dealt(value):
        sent = jnp.einsum("mjs,msd->jmd", deal, value, preferred_element_type=F32)
        return sent.astype(BF16).reshape(seqs, -1, 128)

    def arrived(got):
        return jnp.swapaxes(got.reshape(seq_len, batches, -1), 0, 1)

    tokens_sent = dealt(jnp.concatenate([tokens[:, :, 0], marks], axis=2))
    tokens_got = lax.all_to_all(tokens_sent, DP, 0, 0, tiled=True)
    shards = [
        jnp.concatenate([p[c] for p in attn_parts + ffn_parts], axis=1) for c in (0, 1)
    ]
    core = lax.axis_index("c")
    kept_shard = jnp.where(core == 0, shards[0], shards[1])
    got_shard = swapped(jnp.where(core == 0, shards[1], shards[0]), "c")
    chip_rows = jnp.where(
        core == 0,
        jnp.concatenate([kept_shard, got_shard], axis=0),
        jnp.concatenate([got_shard, kept_shard], axis=0),
    )
    cot_sent = dealt(cotangent[:, :, 0])
    near_w, tokens_got, cot_sent = lax.optimization_barrier(
        (z_gathered(chip_rows), tokens_got, cot_sent)
    )
    attn_w = xy_gathered(near_w[:, :attn_cols])
    ffn_w = xy_gathered(near_w[:, attn_cols:])
    qkv_w, out_w = attn_w[:, :qkv_cols], attn_w[:, qkv_cols:]
    own_in = arrived(tokens_got)
    x_own = dot(own_in[:, :, :width].reshape(batches * seq_len, width), features, (1, 0))
    own_marks = own_in[:, :, width : width + 128]
    own_hits = own_marks[:, :, :experts]
    own_keep = own_marks[:, :, experts].reshape(-1, 1).astype(F32)

    place = jnp.arange(seq_len, dtype=jnp.int32)
    earlier = (place[None, :] < place[:, None]).astype(BF16)
    before = jnp.einsum("pq,mqe->mpe", earlier, own_hits, preferred_element_type=F32)
    totals = jnp.sum(own_hits.astype(F32), axis=1)

    def to_send(own):
        natural = dot(own, features, (1, 1), BF16).reshape(batches, seq_len, -1)
        return jnp.swapaxes(natural, 0, 1).reshape(seq_len, -1, 128)

    def placed(got):
        got = got.reshape(seqs, batches, -1)
        back = jnp.einsum("mjs,jmd->msd", deal, got, preferred_element_type=F32)
        return back.astype(BF16)[:, :, None]

    small_in = to_local(
        jnp.concatenate([gain_attn[None], gain_ffn[None], w_router.T.astype(F32)], axis=0)
    )
    gain_a, gain_f, router = small_in[0:1], small_in[1:2], small_in[2:].astype(BF16)
    scale_attn = lax.rsqrt(jnp.mean(x_own * x_own, axis=-1, keepdims=True) + EPS)
    unit_attn = x_own * scale_attn
    n1_own = (unit_attn * gain_a).astype(BF16)
    n1_own, totals, cot_sent = lax.optimization_barrier((n1_own, totals, cot_sent))
    own_cot = arrived(lax.all_to_all(cot_sent, DP, 0, 0, tiled=True))
    gy_own = own_keep * dot(
        own_cot.reshape(batches * seq_len, width), features, (1, 0)
    )
    other_totals = swapped(totals, "zh")
    rank = before + jnp.where(t == 1, other_totals, 0.0)[:, None, :]
    own_kept = jnp.where(rank < CAP, own_hits, jnp.zeros_like(own_hits))
    flags = (own_hits + own_kept).reshape(batches * seq_len, -1)
    flags = jnp.pad(flags, ((0, 0), (0, 128 - flags.shape[1])))
    gy_own_low = jnp.concatenate([gy_own.astype(BF16), flags], axis=1)
    n1_other, gy_own_low = lax.optimization_barrier((swapped(n1_own, "z0"), gy_own_low))
    n1 = jnp.concatenate([n1_own, n1_other], axis=0)
    n1 = jnp.concatenate([n1, swapped(n1, "c")], axis=0)
    gy_pair = lax.all_to_all(
        jnp.broadcast_to(gy_own_low[None], (2, *gy_own_low.shape)), "z0", 0, 0, tiled=True
    )
    rows = n1.shape[0]
    count = rows // seq_len
    qkv = dot(n1, qkv_w, (1, 0), BF16)
    query = qkv[:, :q_cols].reshape(count, seq_len, GROUP, HEAD_SIZE)
    key = qkv[:, q_cols : q_cols + k_cols].reshape(count, seq_len, HEAD_SIZE)
    value = qkv[:, q_cols + k_cols :].reshape(count, seq_len, HEAD_SIZE)
    scores = attention_scores(query, key)
    log_total = jax.nn.logsumexp(scores, axis=-1, keepdims=True)
    probs = jnp.exp(scores - log_total)
    probs_low = probs.astype(BF16)
    mixed = jnp.einsum("sglm,smd->slgd", probs_low, value, preferred_element_type=F32)
    mixed = mixed.astype(BF16).reshape(rows, q_cols)
    mixed, gy_pair = lax.optimization_barrier((mixed, gy_pair))
    gy_pair = jnp.where(lax.axis_index("z0") == 1, gy_pair[::-1], gy_pair)
    gy_pair = gy_pair.reshape(-1, gy_own_low.shape[1])
    gy_other = swapped(gy_pair, "c")
    h_own = x_own + rows_back(dot(mixed, out_w, (1, 1), BF16))

    scale_ffn = lax.rsqrt(jnp.mean(h_own * h_own, axis=-1, keepdims=True) + EPS)
    unit_ffn = h_own * scale_ffn
    n2_own = (unit_ffn * gain_f).astype(BF16)
    n2_pair = jnp.concatenate([n2_own, swapped(n2_own, "z0")], axis=0)
    n2_other = swapped(n2_pair, "c")
    router_low = jnp.pad(router, ((0, 128 - experts), (0, 0)))
    n2, gy, dab, weighted, dn2_part, out_part, dlogits, small_ffn = experts_both_ways(
        n2_pair, n2_other, gy_pair, gy_other, ffn_w, router_low, experts
    )
    dn2_sum, (dab, weighted) = core_sum(dn2_part, (dab, weighted))
    dn2 = pair_sum(dn2_sum)
    big_down = dot(gy, weighted, (0, 0), BF16)
    big_ffn = jnp.concatenate([dot(n2, dab, (0, 0), BF16), big_down], axis=1)
    small_router = dot(dlogits, n2, (0, 0))[:experts]
    small_ffn = small_ffn / gain_f
    dn2, big_ffn = lax.optimization_barrier((dn2, big_ffn))
    near_ffn = xy_scattered(big_ffn)
    scaled = dn2 * gain_f
    dh = gy_own + scale_ffn * (
        scaled - unit_ffn * jnp.mean(scaled * unit_ffn, axis=-1, keepdims=True)
    )

    dattn_own, out_part = lax.optimization_barrier((dh.astype(BF16), out_part))
    out_halves = z_halves(core_sum(out_part, ())[0].astype(BF16))
    dattn_other, small_router, out_halves = lax.optimization_barrier(
        (swapped(dattn_own, "z0"), small_router, out_halves)
    )
    dattn_pair = jnp.concatenate([dattn_own, dattn_other], axis=0)
    dattn, dqkv, dn1_part, small_attn = attention_backward(
        dattn_pair, swapped(dattn_pair, "c"), qkv, n1, attn_w, seq_len
    )
    dqkv, halves_got = lax.optimization_barrier(
        (dqkv, lax.all_to_all(out_halves, "z0", 0, 0, tiled=True))
    )
    branch = jnp.sum(halves_got.astype(F32), axis=0)
    out_sent = to_send((own_keep * (h_own + branch)).astype(BF16))
    out_got = lax.all_to_all(out_sent, DP, 0, 0, tiled=True)
    small = jnp.concatenate([small_attn / gain_a, small_ffn, small_router], axis=0)
    lines = in_lines(small.astype(BF16), q_cols + qkv_cols)
    big_attn = attention_gradients(n1, dqkv, dattn, mixed, lines, side_x * side_y)
    dn1_sum, big_attn = core_sum(dn1_part, big_attn)
    big_attn, out_got = lax.optimization_barrier((big_attn, out_got))
    dn1 = pair_sum(dn1_sum)
    dn1, near_ffn = lax.optimization_barrier((dn1, near_ffn))
    scaled = dn1 * gain_a
    dx_own = dh + scale_attn * (
        scaled - unit_attn * jnp.mean(scaled * unit_attn, axis=-1, keepdims=True)
    )
    xy_got = lax.all_to_all(big_attn, ("x", "y"), 0, 0, tiled=True)
    ffn_mine = both_cores(z_scattered(near_ffn))
    xy_got, dx_sent, ffn_mine = lax.optimization_barrier(
        (xy_got, to_send(dx_own.astype(BF16)), ffn_mine)
    )
    dx_got = lax.all_to_all(dx_sent, DP, 0, 0, tiled=True)
    summed = jnp.sum(xy_got.astype(F32), axis=0)
    near_attn = summed[:-16].astype(BF16)
    small = to_natural(from_lines(summed[-16:], 2 + experts, width))
    places = len(z_routes())
    lines = jnp.tile(small.reshape(near_attn.shape[0] // places, -1), (places, 1))
    attn_cols = near_attn.shape[1]
    near_attn = jnp.concatenate([near_attn, lines.astype(BF16)], axis=1)
    chip = z_scattered(near_attn)
    attn_mine = both_cores(chip[:, :attn_cols])
    final = chip[:, attn_cols:]
    final = final + swapped(final, "c")
    final = (final + swapped(final, "zh")).reshape(small.shape)
    out_tokens, grad_tokens = placed(out_got), placed(dx_got)
    mine = jnp.concatenate([attn_mine, ffn_mine], axis=2)

    def join(start, cols):
        part = mine[:, :, start : start + cols]
        return jnp.swapaxes(part, 0, 1).reshape(rows_here, 2 * cols)

    def join_experts(start):
        part = mine[:, :, start : start + experts * hidden_e]
        part = part.reshape(2, rows_here, experts, hidden_e)
        return jnp.transpose(part, (2, 1, 0, 3)).reshape(experts, rows_here, 2 * hidden_e)

    shared_cols = s_gate.shape[1] // 2
    ffn_at = attn_cols
    each = experts * hidden_e
    return (
        out_tokens,
        grad_tokens,
        final[0],
        final[1],
        join(0, q_cols),
        join(q_cols, k_cols),
        join(q_cols + k_cols, k_cols),
        join(qkv_cols, q_cols).T,
        final[2:].T,
        join_experts(ffn_at),
        join_experts(ffn_at + hidden),
        jnp.swapaxes(join_experts(ffn_at + 2 * hidden), 1, 2),
        join(ffn_at + each, shared_cols),
        join(ffn_at + hidden + each, shared_cols),
        join(ffn_at + 2 * hidden + each, shared_cols).T,
    )


def solution(mesh):
    devices = np.asarray(mesh.devices)
    side = round((devices.shape[0] // 2) ** (1 / 3))
    fine = Mesh(devices.reshape(side, side // 2, 2, side, 2, 2), EVERY)
    rows, cols = P(DP, "zh"), P("zh", DP)
    seqs = P(None, "zh", DP, None)
    return jax.shard_map(
        on_device,
        mesh=fine,
        in_specs=(
            seqs,
            seqs,
            P(),
            P(),
            P(None, None, DP, None),
            P(),
            P(),
            rows,
            rows,
            rows,
            cols,
            P(),
            P(None, DP, "zh"),
            P(None, DP, "zh"),
            P(None, "zh", DP),
            rows,
            rows,
            cols,
        ),
        out_specs=(
            seqs,
            seqs,
            P(),
            P(),
            rows,
            rows,
            rows,
            cols,
            P(),
            P(None, DP, "zh"),
            P(None, DP, "zh"),
            P(None, "zh", DP),
            rows,
            rows,
            cols,
        ),
        check_vma=False,
    )
```

```python
import math

import jax
import jax.numpy as jnp
import numpy as np
from jax import lax
from jax.experimental import pallas as pl
from jax.experimental.pallas import tpu as pltpu
from jax.sharding import Mesh
from jax.sharding import PartitionSpec as P

QUERY_HEAD_COUNT = 12
KEY_VALUE_HEADS = 4
HEAD_SIZE = 128
GROUP = QUERY_HEAD_COUNT // KEY_VALUE_HEADS
CAP = 128
EPS = 1e-06
DP = ("x", "z1", "z0", "y", "c")
EVERY = ("x", "z1", "z0", "y", "c", "zh")
F32 = jnp.float32
BF16 = jnp.bfloat16


def dot(left, right, contract, out=F32):
    result = lax.dot_general(
        left, right, (((contract[0],), (contract[1],)), ((), ())), preferred_element_type=F32
    )
    return result.astype(out)


def swapped(value, axis, bit=1):
    return lax.ppermute(value, axis, [(i, i ^ bit) for i in range(lax.axis_size(axis))])


def whole_rows(own):
    pair = jnp.concatenate([own, swapped(own, "z0")], axis=0)
    return jnp.concatenate([pair, swapped(pair, "c")], axis=0)


def core_sum(part, tied):
    half = part.shape[0] // 2
    both = part[:half].astype(F32) + swapped(part[half:], "c").astype(F32)
    return lax.optimization_barrier((both, tied))


def pair_sum(both):
    quarter = both.shape[0] // 2
    sent = swapped(both[quarter:].astype(BF16), "z0")
    return both[:quarter] + sent.astype(F32)


def z_halves(both):
    halves = both.reshape(2, -1, both.shape[1])
    return jnp.where(lax.axis_index("z0") == 1, halves[::-1], halves)


def rows_back(part, tied=()):
    return pair_sum(core_sum(part, tied)[0])


def z_routes():
    wide = lax.axis_size("z1")
    found = []
    for k1 in range(wide):
        for k2 in range(2):
            pairs = []
            for z1 in range(wide):
                for z0 in range(2):
                    for zh in range(2):
                        goal = ((z1 ^ k1) * 2 + zh) * 2 + (z0 ^ k2)
                        pairs.append(((z1 * 2 + z0) * 2 + zh, goal))
            found.append(pairs)
    return found


def z_gathered(shard):
    return jnp.concatenate(
        [lax.ppermute(shard, ("z1", "z0", "zh"), pairs) for pairs in z_routes()], axis=0
    )


def z_scattered(near):
    routes = z_routes()
    pieces = near.reshape(len(routes), -1, near.shape[1])
    total = 0.0
    for piece, pairs in zip(pieces, routes):
        back = [(goal, start) for start, goal in pairs]
        total = total + lax.ppermute(piece, ("z1", "z0", "zh"), back).astype(F32)
    return total


def xy_gathered(near):
    return lax.all_gather(near, ("x", "y"), axis=0, tiled=True)


def xy_scattered(total):
    return lax.psum_scatter(total, ("x", "y"), scatter_dimension=0, tiled=True)


def in_lines(small, cols):
    first = min(small.shape[1], cols)
    lines = jnp.pad(small[:, :first], ((0, 0), (0, cols - first)))
    lines = jnp.concatenate([lines, small[:, first:].reshape(-1, cols)], axis=0)
    return jnp.pad(lines, ((0, 16 - lines.shape[0]), (0, 0)))


def from_lines(lines, rows, width):
    first = min(width, lines.shape[1])
    rest = lines[rows : rows + rows * (width - first) // lines.shape[1]]
    return jnp.concatenate([lines[:rows, :first], rest.reshape(rows, -1)], axis=1)


def expert_kernel(
    experts,
    n2_pair_ref,
    n2_other_ref,
    gy_pair_ref,
    gy_other_ref,
    w_ref,
    router_ref,
    n2_ref,
    gy_ref,
    dab_ref,
    weighted_ref,
    dn2_ref,
    out_ref,
    dlogits_ref,
    small_ref,
):
    hidden = weighted_ref.shape[1]
    each = hidden // (experts + 2)
    width = n2_ref.shape[1]
    second = pl.program_id(0) * 2 >= pl.num_programs(0)
    n2 = jnp.where(second, n2_other_ref[...], n2_pair_ref[...])
    gy = jnp.where(second, gy_other_ref[:, :width], gy_pair_ref[:, :width])
    flags = jnp.where(second, gy_other_ref[:, width:], gy_pair_ref[:, width:]).astype(F32)
    n2_ref[...] = n2
    gy_ref[...] = gy
    named, kept = flags > 0.5, flags > 1.5
    logits = dot(n2, router_ref[...], (1, 1))
    top = jnp.max(jnp.where(named, logits, -1e30), axis=1, keepdims=True)
    powers = jnp.where(named, jnp.exp(jnp.where(named, logits - top, 0.0)), 0.0)
    gates = powers / jnp.maximum(jnp.sum(powers, axis=1, keepdims=True), 1e-30)
    kept_gates = jnp.where(kept, gates, 0.0)
    lane = lax.broadcasted_iota(jnp.int32, flags.shape, 1)
    dgates = jnp.zeros(flags.shape, F32)
    step = 2 * each
    for at in range(0, hidden, step):
        a = dot(n2, w_ref[:, at : at + step], (1, 0))
        b = dot(n2, w_ref[:, hidden + at : hidden + at + step], (1, 0))
        dhid = dot(gy, w_ref[:, 2 * hidden + at : 2 * hidden + at + step], (1, 0))
        sigma = 1.0 / (1.0 + jnp.exp(-a))
        silu = a * sigma
        inner = (silu * b).astype(BF16).astype(F32)
        first = at // each
        if first < experts:
            scale = jnp.concatenate(
                [
                    jnp.broadcast_to(kept_gates[:, e : e + 1], (flags.shape[0], each))
                    for e in (first, first + 1)
                ],
                axis=1,
            )
            product = inner * dhid
            for e in (first, first + 1):
                lo = (e - first) * each
                total = jnp.sum(product[:, lo : lo + each], axis=1, keepdims=True)
                dgates = jnp.where(lane == e, total, dgates)
            weighted = scale * inner
            dinner = scale * dhid
        else:
            weighted, dinner = inner, dhid
        weighted_ref[:, at : at + step] = weighted.astype(BF16)
        slope = sigma * (1.0 + a * (1.0 - sigma))
        dab_ref[:, at : at + step] = (dinner * b * slope).astype(BF16)
        dab_ref[:, hidden + at : hidden + at + step] = (dinner * silu).astype(BF16)
    dgates = jnp.where(kept, dgates, 0.0)
    dlogits = gates * (dgates - jnp.sum(gates * dgates, axis=1, keepdims=True))
    dlogits = dlogits.astype(BF16)
    dlogits_ref[...] = dlogits
    tile = width // 3
    dab = dab_ref[...]
    weighted = weighted_ref[...]

    @pl.when(pl.program_id(0) == 0)
    def _():
        small_ref[...] = jnp.zeros_like(small_ref)

    for at in range(0, width, tile):
        dn2 = dot(dab, w_ref[at : at + tile, : 2 * hidden], (1, 1))
        dn2 = dn2 + dot(dlogits, router_ref[:, at : at + tile], (1, 0))
        dn2_ref[:, at : at + tile] = dn2.astype(BF16)
        small_ref[:, at : at + tile] += jnp.sum(
            dn2 * n2_ref[:, at : at + tile].astype(F32), axis=0, keepdims=True
        )
        out_ref[:, at : at + tile] = dot(
            weighted, w_ref[at : at + tile, 2 * hidden :], (1, 1), BF16
        )


def experts_both_ways(n2_pair, n2_other, gy_pair, gy_other, ffn_w, router, experts):
    half, width = n2_pair.shape
    rows = 2 * half
    tile = half // 2
    hidden = ffn_w.shape[1] // 3

    def first_half(cols):
        return pl.BlockSpec((tile, cols), lambda i: (jnp.minimum(i, 1), 0))

    def second_half(cols):
        return pl.BlockSpec((tile, cols), lambda i: (jnp.maximum(i - 2, 0), 0))

    def by_tile(cols):
        return pl.BlockSpec((tile, cols), lambda i: (i, 0))

    operands = (n2_pair, n2_other, gy_pair, gy_other, ffn_w, router)
    shapes = (width, width, 2 * hidden, hidden, width, width, 128)
    return pl.pallas_call(
        lambda *refs: expert_kernel(experts, *refs),
        grid=(4,),
        in_specs=[
            first_half(width),
            second_half(width),
            first_half(gy_pair.shape[1]),
            second_half(gy_pair.shape[1]),
        ]
        + [
            pl.BlockSpec(v.shape, lambda i: (0, 0), pipeline_mode=pl.Buffered(1))
            for v in operands[4:]
        ],
        out_specs=[by_tile(n) for n in shapes] + [pl.BlockSpec((1, width), lambda i: (0, 0))],
        out_shape=[jax.ShapeDtypeStruct((rows, n), BF16) for n in shapes]
        + [jax.ShapeDtypeStruct((1, width), F32)],
        compiler_params=pltpu.CompilerParams(vmem_limit_bytes=54 << 20),
        cost_estimate=pl.CostEstimate(
            flops=12 * rows * width * hidden,
            transcendentals=2 * rows * hidden,
            bytes_accessed=2 * (ffn_w.size + rows * (8 * width + 3 * hidden)),
        ),
        name="experts",
    )(*operands)


def attention_backward_kernel(
    seq_len,
    pair_ref,
    other_ref,
    qkv_ref,
    n1_ref,
    w_ref,
    dattn_ref,
    dqkv_ref,
    dn1_ref,
    small_ref,
):
    tile, width = dattn_ref.shape
    cols = dqkv_ref.shape[1]
    q_cols = GROUP * HEAD_SIZE
    root = 1.0 / math.sqrt(HEAD_SIZE)
    dattn = jnp.where(pl.program_id(0) == 1, other_ref[...], pair_ref[...])
    dattn_ref[...] = dattn
    dmixed = dot(dattn, w_ref[:, cols:], (1, 0), BF16)
    row = lax.broadcasted_iota(jnp.int32, (seq_len, seq_len), 0)
    seen = lax.broadcasted_iota(jnp.int32, (seq_len, seq_len), 1) <= row
    for start in range(0, tile, seq_len):
        at = slice(start, start + seq_len)
        key = qkv_ref[at, q_cols : q_cols + HEAD_SIZE]
        value = qkv_ref[at, q_cols + HEAD_SIZE :]
        dkey = jnp.zeros((seq_len, HEAD_SIZE), F32)
        dvalue = jnp.zeros((seq_len, HEAD_SIZE), F32)
        for head in range(0, q_cols, HEAD_SIZE):
            query = qkv_ref[at, head : head + HEAD_SIZE]
            grad = dmixed[at, head : head + HEAD_SIZE]
            scores = jnp.where(seen, dot(query, key, (1, 1)) * root, -1e30)
            powers = jnp.exp(scores - jnp.max(scores, axis=1, keepdims=True))
            probs = powers / jnp.sum(powers, axis=1, keepdims=True)
            dprobs = dot(grad, value, (1, 1))
            inside = jnp.sum(probs * dprobs, axis=1, keepdims=True)
            dscores = (probs * (dprobs - inside)).astype(BF16)
            dqkv_ref[at, head : head + HEAD_SIZE] = (dot(dscores, key, (1, 0)) * root).astype(BF16)
            dkey = dkey + dot(dscores, query, (0, 0))
            dvalue = dvalue + dot(probs.astype(BF16), grad, (0, 0))
        dqkv_ref[at, q_cols : q_cols + HEAD_SIZE] = (dkey * root).astype(BF16)
        dqkv_ref[at, q_cols + HEAD_SIZE :] = dvalue.astype(BF16)
    dqkv = dqkv_ref[...]

    @pl.when(pl.program_id(0) == 0)
    def _():
        small_ref[...] = jnp.zeros_like(small_ref)

    step = width // 3
    for at in range(0, width, step):
        dn1 = dot(dqkv, w_ref[at : at + step, :cols], (1, 1))
        dn1_ref[:, at : at + step] = dn1.astype(BF16)
        small_ref[:, at : at + step] += jnp.sum(
            dn1 * n1_ref[:, at : at + step].astype(F32), axis=0, keepdims=True
        )


def attention_backward(pair, other, qkv, n1, attn_w, seq_len):
    tile, width = pair.shape
    rows, cols = qkv.shape

    def whole(value):
        return pl.BlockSpec(value.shape, lambda i: (0, 0), pipeline_mode=pl.Buffered(1))

    def by_tile(cols):
        return pl.BlockSpec((tile, cols), lambda i: (i, 0))

    return pl.pallas_call(
        lambda *refs: attention_backward_kernel(seq_len, *refs),
        grid=(2,),
        in_specs=[whole(pair), whole(other), by_tile(cols), by_tile(width), whole(attn_w)],
        out_specs=[
            by_tile(width),
            by_tile(cols),
            by_tile(width),
            pl.BlockSpec((1, width), lambda i: (0, 0)),
        ],
        out_shape=[jax.ShapeDtypeStruct((rows, n), BF16) for n in (width, cols, width)]
        + [jax.ShapeDtypeStruct((1, width), F32)],
        compiler_params=pltpu.CompilerParams(vmem_limit_bytes=44 << 20),
        cost_estimate=pl.CostEstimate(
            flops=12 * rows * width * attn_w.shape[1],
            transcendentals=rows * seq_len * GROUP,
            bytes_accessed=2 * (attn_w.size + rows * (5 * width + 2 * cols)),
        ),
        name="attention_backward",
    )(pair, other, qkv, n1, attn_w)


def gradients_kernel(n1_ref, dattn_ref, dqkv_ref, mixed_ref, lines_ref, out_ref):
    blocks = out_ref.shape[0]
    rows = n1_ref.shape[1] // blocks
    split = dqkv_ref.shape[1]
    qkv = dot(n1_ref[...], dqkv_ref[...], (0, 0), BF16)
    out = dot(dattn_ref[...], mixed_ref[...], (0, 0), BF16)
    for b in range(blocks):
        out_ref[b, :rows, :split] = qkv[b * rows : (b + 1) * rows]
        out_ref[b, :rows, split:] = out[b * rows : (b + 1) * rows]
        out_ref[b, rows:, :] = lines_ref[...]


def attention_gradients(n1, dqkv, dattn, mixed, small, places):
    rows, width = n1.shape
    cols = dqkv.shape[1] + mixed.shape[1]
    lines = width // places + small.shape[0]
    step = width // 4

    def whole(value):
        return pl.BlockSpec(value.shape, lambda i: (0, 0), pipeline_mode=pl.Buffered(1))

    by_features = pl.BlockSpec((rows, step), lambda i: (0, i))
    return pl.pallas_call(
        gradients_kernel,
        grid=(4,),
        in_specs=[by_features, by_features, whole(dqkv), whole(mixed), whole(small)],
        out_specs=pl.BlockSpec((places // 4, lines, cols), lambda i: (i, 0, 0)),
        out_shape=jax.ShapeDtypeStruct((places, lines, cols), BF16),
        compiler_params=pltpu.CompilerParams(vmem_limit_bytes=40 << 20),
        cost_estimate=pl.CostEstimate(
            flops=2 * rows * width * cols,
            transcendentals=0,
            bytes_accessed=2 * (2 * rows * width + rows * cols + places * lines * cols),
        ),
        name="attention_gradients",
    )(n1, dattn, dqkv, mixed, small)


def norm_backward_kernel(sum_ref, got_ref, value_ref, scale_ref, gain_ref, grad_ref, out_ref, low_ref):
    unit = value_ref[...] * scale_ref[...]
    scaled = (sum_ref[...] + got_ref[...].astype(F32)) * gain_ref[...]
    inside = jnp.mean(scaled * unit, axis=1, keepdims=True)
    out = grad_ref[...].astype(F32) + scale_ref[...] * (scaled - unit * inside)
    out_ref[...] = out
    low_ref[...] = out.astype(BF16)


def norm_backward(both, got, value, scale, gain, grad):
    rows, width = got.shape
    tile = rows // 4

    def by_tile(cols):
        return pl.BlockSpec((tile, cols), lambda i: (i, 0))

    return pl.pallas_call(
        norm_backward_kernel,
        grid=(4,),
        in_specs=[
            by_tile(width),
            by_tile(width),
            by_tile(width),
            by_tile(1),
            pl.BlockSpec((1, width), lambda i: (0, 0)),
            by_tile(width),
        ],
        out_specs=[by_tile(width), by_tile(width)],
        out_shape=[
            jax.ShapeDtypeStruct((rows, width), F32),
            jax.ShapeDtypeStruct((rows, width), BF16),
        ],
        cost_estimate=pl.CostEstimate(
            flops=10 * rows * width, transcendentals=0, bytes_accessed=18 * rows * width
        ),
        name="norm_backward",
    )(both, got, value, scale, gain, grad)


def attention_scores(query, key):
    scaled = jnp.einsum("slgd,smd->sglm", query, key, preferred_element_type=F32) * (
        1.0 / math.sqrt(HEAD_SIZE)
    )
    place = jnp.arange(query.shape[1], dtype=jnp.int32)
    return jnp.where(place[None, :] <= place[:, None], scaled, -1e30)


def on_device(
    tokens,
    cotangent,
    lengths,
    perm,
    routes,
    gain_attn,
    gain_ffn,
    query_matrix,
    key_matrix,
    value_matrix,
    w_out,
    w_router,
    w_gate,
    w_up,
    w_down,
    s_gate,
    s_up,
    s_down,
):
    t = lax.axis_index("zh")
    place_here = lax.axis_index(DP)
    side_x, side_z1, side_z0, side_y = (lax.axis_size(a) for a in ("x", "z1", "z0", "y"))
    side_zl = side_z1 * side_z0
    flips = (lax.axis_index("z1"), t)
    batches, seqs = tokens.shape[0], tokens.shape[1]
    seq_len = lax.axis_size(DP)
    width = tokens.shape[3]
    experts = w_gate.shape[0]
    rows_here = query_matrix.shape[0]

    def halves(value):
        cols = value.shape[-1] // 2
        return value[..., :cols], value[..., cols:]

    def by_row(value):
        return jnp.concatenate([value[e] for e in range(experts)], axis=1)

    attn_parts = [halves(v) for v in (query_matrix, key_matrix, value_matrix, w_out.T)]
    ffn_parts = [
        tuple(by_row(v) for v in halves(w_gate)),
        halves(s_gate),
        tuple(by_row(v) for v in halves(w_up)),
        halves(s_up),
        tuple(by_row(v) for v in halves(jnp.swapaxes(w_down, 1, 2))),
        halves(s_down.T),
    ]
    attn_cols = sum(p[0].shape[1] for p in attn_parts)
    q_cols = query_matrix.shape[1] // 2
    k_cols = key_matrix.shape[1] // 2
    qkv_cols = q_cols + 2 * k_cols
    hidden_e = w_gate.shape[2] // 2
    hidden = experts * hidden_e + s_gate.shape[1] // 2

    def flipped(value, axes):
        for axis, flip in zip(axes, flips):
            value = jnp.where(flip == 1, jnp.flip(value, axis), value)
        return value

    def to_local(value):
        parts = value.reshape(-1, side_x, side_z1, side_z0, side_y, width // (seq_len // 2))
        return flipped(jnp.transpose(parts, (0, 1, 4, 2, 3, 5)), (3, 4)).reshape(value.shape)

    def to_natural(value):
        parts = value.reshape(-1, side_x, side_y, side_z1, side_z0, width // (seq_len // 2))
        return jnp.transpose(flipped(parts, (3, 4)), (0, 1, 3, 4, 2, 5)).reshape(value.shape)

    unit = width // (seq_len // 2)
    iota = jnp.arange(width, dtype=jnp.int32)
    piece = iota // unit
    zl_of = (piece % side_zl) ^ (flips[0] * 2 + flips[1])
    mate = (
        ((piece // (side_zl * side_y)) * side_zl + zl_of) * side_y + (piece // side_zl) % side_y
    ) * unit + iota % unit
    features = (iota[:, None] == mate[None, :]).astype(BF16)

    def both_cores(chip):
        low = chip.astype(BF16)
        kept = jnp.where(core == 0, low[:rows_here], low[rows_here:])
        got = swapped(jnp.where(core == 0, low[rows_here:], low[:rows_here]), "c")
        pair = jnp.where(core == 0, jnp.stack([kept, got]), jnp.stack([got, kept]))
        return pair.astype(F32)

    order = lax.dynamic_index_in_dim(perm, t, 1, False)
    deal = (order[:, :, None] == jnp.arange(seqs, dtype=jnp.int32)[None, None, :]).astype(BF16)
    own_routes = lax.dynamic_slice_in_dim(routes[:, :, 0], t * seqs, seqs, 1)
    own_lengths = lax.dynamic_slice_in_dim(lengths, t * seqs, seqs, 1)
    own_valid = place_here < own_lengths
    named = jnp.any(
        own_routes[:, :, :, None] == jnp.arange(experts, dtype=jnp.int32), axis=2
    )
    marks = jnp.concatenate(
        [jnp.logical_and(named, own_valid[:, :, None]), own_valid[:, :, None]], axis=2
    ).astype(BF16)
    marks = jnp.pad(marks, ((0, 0), (0, 0), (0, 128 - marks.shape[2])))

    def dealt(value):
        sent = jnp.einsum("mjs,msd->jmd", deal, value, preferred_element_type=F32)
        return sent.astype(BF16).reshape(seqs, -1, 128)

    def arrived(got):
        return jnp.swapaxes(got.reshape(seq_len, batches, -1), 0, 1)

    tokens_sent = dealt(jnp.concatenate([tokens[:, :, 0], marks], axis=2))
    tokens_got = lax.all_to_all(tokens_sent, DP, 0, 0, tiled=True)
    shards = [
        jnp.concatenate([p[c] for p in attn_parts + ffn_parts], axis=1) for c in (0, 1)
    ]
    core = lax.axis_index("c")
    kept_shard = jnp.where(core == 0, shards[0], shards[1])
    got_shard = swapped(jnp.where(core == 0, shards[1], shards[0]), "c")
    chip_rows = jnp.where(
        core == 0,
        jnp.concatenate([kept_shard, got_shard], axis=0),
        jnp.concatenate([got_shard, kept_shard], axis=0),
    )
    cot_sent = dealt(cotangent[:, :, 0])
    near_w, tokens_got, cot_sent = lax.optimization_barrier(
        (z_gathered(chip_rows), tokens_got, cot_sent)
    )
    attn_w = xy_gathered(near_w[:, :attn_cols])
    ffn_w = xy_gathered(near_w[:, attn_cols:])
    qkv_w, out_w = attn_w[:, :qkv_cols], attn_w[:, qkv_cols:]
    own_in = arrived(tokens_got)
    x_own = dot(own_in[:, :, :width].reshape(batches * seq_len, width), features, (1, 0))
    own_marks = own_in[:, :, width : width + 128]
    own_hits = own_marks[:, :, :experts]
    own_keep = own_marks[:, :, experts].reshape(-1, 1).astype(F32)

    place = jnp.arange(seq_len, dtype=jnp.int32)
    earlier = (place[None, :] < place[:, None]).astype(BF16)
    before = jnp.einsum("pq,mqe->mpe", earlier, own_hits, preferred_element_type=F32)
    totals = jnp.sum(own_hits.astype(F32), axis=1)

    def to_send(own):
        natural = dot(own, features, (1, 1), BF16).reshape(batches, seq_len, -1)
        return jnp.swapaxes(natural, 0, 1).reshape(seq_len, -1, 128)

    def placed(got):
        got = got.reshape(seqs, batches, -1)
        back = jnp.einsum("mjs,jmd->msd", deal, got, preferred_element_type=F32)
        return back.astype(BF16)[:, :, None]

    small_in = to_local(
        jnp.concatenate([gain_attn[None], gain_ffn[None], w_router.T.astype(F32)], axis=0)
    )
    gain_a, gain_f, router = small_in[0:1], small_in[1:2], small_in[2:].astype(BF16)
    scale_attn = lax.rsqrt(jnp.mean(x_own * x_own, axis=-1, keepdims=True) + EPS)
    unit_attn = x_own * scale_attn
    n1_own = (unit_attn * gain_a).astype(BF16)
    n1_own, totals, cot_sent = lax.optimization_barrier((n1_own, totals, cot_sent))
    own_cot = arrived(lax.all_to_all(cot_sent, DP, 0, 0, tiled=True))
    gy_own = own_keep * dot(
        own_cot.reshape(batches * seq_len, width), features, (1, 0)
    )
    other_totals = swapped(totals, "zh")
    rank = before + jnp.where(t == 1, other_totals, 0.0)[:, None, :]
    own_kept = jnp.where(rank < CAP, own_hits, jnp.zeros_like(own_hits))
    flags = (own_hits + own_kept).reshape(batches * seq_len, -1)
    flags = jnp.pad(flags, ((0, 0), (0, 128 - flags.shape[1])))
    gy_own_low = jnp.concatenate([gy_own.astype(BF16), flags], axis=1)
    n1_other, gy_own_low = lax.optimization_barrier((swapped(n1_own, "z0"), gy_own_low))
    n1 = jnp.concatenate([n1_own, n1_other], axis=0)
    n1 = jnp.concatenate([n1, swapped(n1, "c")], axis=0)
    gy_pair = lax.all_to_all(
        jnp.broadcast_to(gy_own_low[None], (2, *gy_own_low.shape)), "z0", 0, 0, tiled=True
    )
    rows = n1.shape[0]
    count = rows // seq_len
    qkv = dot(n1, qkv_w, (1, 0), BF16)
    query = qkv[:, :q_cols].reshape(count, seq_len, GROUP, HEAD_SIZE)
    key = qkv[:, q_cols : q_cols + k_cols].reshape(count, seq_len, HEAD_SIZE)
    value = qkv[:, q_cols + k_cols :].reshape(count, seq_len, HEAD_SIZE)
    scores = attention_scores(query, key)
    log_total = jax.nn.logsumexp(scores, axis=-1, keepdims=True)
    probs = jnp.exp(scores - log_total)
    probs_low = probs.astype(BF16)
    mixed = jnp.einsum("sglm,smd->slgd", probs_low, value, preferred_element_type=F32)
    mixed = mixed.astype(BF16).reshape(rows, q_cols)
    mixed, gy_pair = lax.optimization_barrier((mixed, gy_pair))
    gy_pair = jnp.where(lax.axis_index("z0") == 1, gy_pair[::-1], gy_pair)
    gy_pair = gy_pair.reshape(-1, gy_own_low.shape[1])
    gy_other = swapped(gy_pair, "c")
    h_own = x_own + rows_back(dot(mixed, out_w, (1, 1), BF16))

    scale_ffn = lax.rsqrt(jnp.mean(h_own * h_own, axis=-1, keepdims=True) + EPS)
    unit_ffn = h_own * scale_ffn
    n2_own = (unit_ffn * gain_f).astype(BF16)
    n2_pair = jnp.concatenate([n2_own, swapped(n2_own, "z0")], axis=0)
    n2_other = swapped(n2_pair, "c")
    router_low = jnp.pad(router, ((0, 128 - experts), (0, 0)))
    n2, gy, dab, weighted, dn2_part, out_part, dlogits, small_ffn = experts_both_ways(
        n2_pair, n2_other, gy_pair, gy_other, ffn_w, router_low, experts
    )
    dn2_sum, (dab, weighted) = core_sum(dn2_part, (dab, weighted))
    quarter = dn2_sum.shape[0] // 2
    dn2_got = swapped(dn2_sum[quarter:].astype(BF16), "z0")
    big_down = dot(gy, weighted, (0, 0), BF16)
    big_ffn = jnp.concatenate([dot(n2, dab, (0, 0), BF16), big_down], axis=1)
    small_router = dot(dlogits, n2, (0, 0))[:experts]
    small_ffn = small_ffn / gain_f
    dn2_got, big_ffn = lax.optimization_barrier((dn2_got, big_ffn))
    near_ffn = xy_scattered(big_ffn)
    dh, dattn_own = norm_backward(dn2_sum, dn2_got, h_own, scale_ffn, gain_f, gy_own_low[:, :width])

    dattn_own, out_part = lax.optimization_barrier((dattn_own, out_part))
    out_halves = z_halves(core_sum(out_part, ())[0].astype(BF16))
    dattn_other, small_router, out_halves = lax.optimization_barrier(
        (swapped(dattn_own, "z0"), small_router, out_halves)
    )
    dattn_pair = jnp.concatenate([dattn_own, dattn_other], axis=0)
    dattn, dqkv, dn1_part, small_attn = attention_backward(
        dattn_pair, swapped(dattn_pair, "c"), qkv, n1, attn_w, seq_len
    )
    dqkv, halves_got = lax.optimization_barrier(
        (dqkv, lax.all_to_all(out_halves, "z0", 0, 0, tiled=True))
    )
    branch = jnp.sum(halves_got.astype(F32), axis=0)
    out_sent = to_send((own_keep * (h_own + branch)).astype(BF16))
    out_got = lax.all_to_all(out_sent, DP, 0, 0, tiled=True)
    small = jnp.concatenate([small_attn / gain_a, small_ffn, small_router], axis=0)
    lines = in_lines(small.astype(BF16), q_cols + qkv_cols)
    big_attn = attention_gradients(n1, dqkv, dattn, mixed, lines, side_x * side_y)
    dn1_sum, big_attn = core_sum(dn1_part, big_attn)
    big_attn, out_got = lax.optimization_barrier((big_attn, out_got))
    dn1 = pair_sum(dn1_sum)
    dn1, near_ffn = lax.optimization_barrier((dn1, near_ffn))
    scaled = dn1 * gain_a
    dx_own = dh + scale_attn * (
        scaled - unit_attn * jnp.mean(scaled * unit_attn, axis=-1, keepdims=True)
    )
    xy_got = lax.all_to_all(big_attn, ("x", "y"), 0, 0, tiled=True)
    ffn_mine = both_cores(z_scattered(near_ffn))
    xy_got, dx_sent, ffn_mine = lax.optimization_barrier(
        (xy_got, to_send(dx_own.astype(BF16)), ffn_mine)
    )
    dx_got = lax.all_to_all(dx_sent, DP, 0, 0, tiled=True)
    summed = jnp.sum(xy_got.astype(F32), axis=0)
    near_attn = summed[:-16].astype(BF16)
    small = to_natural(from_lines(summed[-16:], 2 + experts, width))
    places = len(z_routes())
    lines = jnp.tile(small.reshape(near_attn.shape[0] // places, -1), (places, 1))
    attn_cols = near_attn.shape[1]
    near_attn = jnp.concatenate([near_attn, lines.astype(BF16)], axis=1)
    chip = z_scattered(near_attn)
    attn_mine = both_cores(chip[:, :attn_cols])
    final = chip[:, attn_cols:]
    final = final + swapped(final, "c")
    final = (final + swapped(final, "zh")).reshape(small.shape)
    out_tokens, grad_tokens = placed(out_got), placed(dx_got)
    mine = jnp.concatenate([attn_mine, ffn_mine], axis=2)

    def join(start, cols):
        part = mine[:, :, start : start + cols]
        return jnp.swapaxes(part, 0, 1).reshape(rows_here, 2 * cols)

    def join_experts(start):
        part = mine[:, :, start : start + experts * hidden_e]
        part = part.reshape(2, rows_here, experts, hidden_e)
        return jnp.transpose(part, (2, 1, 0, 3)).reshape(experts, rows_here, 2 * hidden_e)

    shared_cols = s_gate.shape[1] // 2
    ffn_at = attn_cols
    each = experts * hidden_e
    return (
        out_tokens,
        grad_tokens,
        final[0],
        final[1],
        join(0, q_cols),
        join(q_cols, k_cols),
        join(q_cols + k_cols, k_cols),
        join(qkv_cols, q_cols).T,
        final[2:].T,
        join_experts(ffn_at),
        join_experts(ffn_at + hidden),
        jnp.swapaxes(join_experts(ffn_at + 2 * hidden), 1, 2),
        join(ffn_at + each, shared_cols),
        join(ffn_at + hidden + each, shared_cols),
        join(ffn_at + 2 * hidden + each, shared_cols).T,
    )


def solution(mesh):
    devices = np.asarray(mesh.devices)
    side = round((devices.shape[0] // 2) ** (1 / 3))
    fine = Mesh(devices.reshape(side, side // 2, 2, side, 2, 2), EVERY)
    rows, cols = P(DP, "zh"), P("zh", DP)
    seqs = P(None, "zh", DP, None)
    return jax.shard_map(
        on_device,
        mesh=fine,
        in_specs=(
            seqs,
            seqs,
            P(),
            P(),
            P(None, None, DP, None),
            P(),
            P(),
            rows,
            rows,
            rows,
            cols,
            P(),
            P(None, DP, "zh"),
            P(None, DP, "zh"),
            P(None, "zh", DP),
            rows,
            rows,
            cols,
        ),
        out_specs=(
            seqs,
            seqs,
            P(),
            P(),
            rows,
            rows,
            rows,
            cols,
            P(),
            P(None, DP, "zh"),
            P(None, DP, "zh"),
            P(None, "zh", DP),
            rows,
            rows,
            cols,
        ),
        check_vma=False,
    )
```
